32 devices in a mesh: ctx: 4 (over y, x), exp: 8 (over z, core).
Axes of the slice: x: 2, y: 2, z: 4, core: 2. Of those that a mesh axis runs over, the one named last changes fastest.
Arguments:
- states: bfloat16 [8, 128, 2560], P('exp'), may hold values from -13 to 13
- out_grad: bfloat16 [8, 128, 2560], P('exp'), may hold values from -6 to 6
- doc_keys: bfloat16 [8, 512, 2560], P('exp', 'ctx'), may hold values from -60 to 60
- doc_values: bfloat16 [8, 512, 2560], P('exp', 'ctx'), may hold values from -18 to 18
- norm_gain: float32 [2560], replicated, may hold values from 0.5 to 1.5
- expert_ids: int32 [8, 128, 2], P('exp'), may hold values from 0 to 7, all different within a row; in each aligned block of 128 rows (0 to 127, 128 to 255, ..., all dimensions but the last counted through in order) at most 40 rows name the same one
- gate_values: float32 [8, 128, 2], P('exp'), may hold values from 0.5 to 2.5
- expert_weights: bfloat16 [8, 2048, 2, 2560], P('exp', 'ctx'), may hold values from -0.125 to 0.125
Outputs:
- states_grad: bfloat16 [8, 128, 2560], P('exp')
- keys_grad: bfloat16 [8, 512, 2560], P('exp', 'ctx')
- values_grad: bfloat16 [8, 512, 2560], P('exp', 'ctx')
- weights_grad: bfloat16 [8, 2048, 2, 2560], P('exp', 'ctx')
The draws below stay inside these ranges and needn't reach their ends.
Inputs may be any that keep to these rules, and one draw needn't show every extreme that they name: `expert_ids`: within one sequence's 128 tokens, every expert is named by at most 40 tokens.
All inputs are finite; a program needn't handle non-finite values.
Results may differ from the reference program's by a relative error of at most 0.04.
Values may be sent and summed in bfloat16 or wider, within the bound.
A program may use at most 128 MiB of HBM per device.

```python
import math
import jax
import jax.numpy as jnp
import numpy as np
from jax import lax

HEADS = 20
HEAD = 128
D = 2560
EXPERT_FF = 2048
TOP = 2
EXPERTS = 8
DEC_DEV = 128
SEQS = 8
DOC_LEN = 512
CAP = 40
N_CTX = 4


def shared_states(key):
    base = jax.random.normal(jax.random.fold_in(key, 11), (SEQS, DEC_DEV, D), jnp.float32)
    return jnp.clip(base, -4.5, 4.5)


def draw_states(key, part):
    return shared_states(key).astype(jnp.bfloat16)


def draw_doc_keys(key, part):
    noise = jax.random.normal(jax.random.fold_in(key, 23), (SEQS, DOC_LEN, D), jnp.float32)
    noise = jnp.clip(noise, -6.0, 6.0) * 2.0
    return noise.astype(jnp.bfloat16)


def steps_of(own_key, shape, cuts, low, top_value):
    level = 1.0
    for axis_at, parts in cuts:
        draws = jax.random.uniform(jax.random.fold_in(jax.random.fold_in(own_key, 6), axis_at), (parts,), jnp.float32, low / len(cuts), top_value / len(cuts))
        level = level * jnp.repeat(jnp.exp(draws), shape[axis_at] // parts).reshape((-1,) + (1,) * (len(shape) - 1 - axis_at))
    return level


def assign_block(rng, own, number, rows, number_of, top, limit, slope):
    ranking = jax.random.permutation(rng, number_of)
    heavy_load, usual = load_shares(number_of, rows * top, limit, slope, True), load_shares(number_of, rows * top, limit, slope, False)
    places = jnp.arange(number_of)

    def named(sizes, offset_by):
        used = int((sizes > 0).sum())
        fixed = max(1, used // 4)
        shifted = fixed + (places - fixed + offset_by * (used - fixed)) % max(1, number_of - fixed)
        return jnp.zeros((number_of,), jnp.int32).at[ranking[jnp.where(places < fixed, places, shifted)]].set(jnp.asarray(sizes, jnp.int32))

    sizes = jnp.where(number % 4 == 0, named(heavy_load, number // 4), named(usual, number - number // 4 - 1))
    mixed = jax.random.permutation(jax.random.fold_in(own, 3), number_of)
    source_of, receiver = mixed[0:number_of // 2 * 2:2], mixed[1:number_of // 2 * 2:2]
    room = jnp.minimum(sizes[source_of] - 1, limit - sizes[receiver]) // 2
    room = jnp.where((source_of == ranking[0]) | (receiver == ranking[0]) | (sizes[receiver] == 0), 0, jnp.maximum(room, 0))
    shifted = jax.random.randint(jax.random.fold_in(own, 4), (number_of // 2,), 0, 1 << 20) % (room + 1)
    sizes = sizes.at[source_of].add(-shifted).at[receiver].add(shifted)
    items = jnp.searchsorted(jnp.cumsum(sizes), jnp.arange(rows * top), side="right").astype(jnp.int32)
    grid = items.reshape(top, rows).T
    grid = grid[jax.random.permutation(jax.random.fold_in(own, 1), rows)]
    offset_by = jax.random.randint(jax.random.fold_in(own, 2), (rows, 1), 0, top)
    return jnp.take_along_axis(grid, (jnp.arange(top)[None, :] + offset_by) % top, axis=1)


def load_shares(number_of, total, reach, slope, full):
    loads = [(1 << 20) // math.isqrt(rank ** slope) + 1 for rank in range(1, number_of + 1)]
    largest = reach if full else min(reach, max(-(-total // number_of), total * loads[0] // sum(loads)))
    least = 1 if total - largest >= number_of - 1 else 0
    holding, surplus = [largest] + [least] * (number_of - 1), total - largest - least * (number_of - 1)
    while surplus > 0:
        candidates = [i for i in range(1, number_of) if holding[i] < largest] or [i for i in range(1, number_of) if holding[i] < reach]
        pool, remaining = sum([loads[i] for i in candidates]), surplus
        for i in candidates:
            extra = min(reach - holding[i], max(1, remaining * loads[i] // pool), surplus)
            holding[i] = holding[i] + extra
            surplus = surplus - extra
    return np.array(holding)


def bell_draw(rng, dims, scale, limit, shards=(), kind=jnp.bfloat16):
    result = scale * jax.random.normal(rng, dims, jnp.float32)
    if shards:
        result = result * steps_of(rng, dims, shards, -0.22, 0.18)
    return jnp.clip(result, -limit, limit).astype(kind)


def setup_inputs(seed: int = 0) -> dict:
    splits = jax.random.split(jax.random.key(seed), 9)
    states = draw_states(jax.random.fold_in(splits[8], 71), 0)
    out_grad = bell_draw(splits[1], (SEQS, DEC_DEV, D), 1.0, 6.0, ((0, 8),))
    doc_keys = draw_doc_keys(jax.random.fold_in(splits[8], 71), 0)
    doc_values = bell_draw(splits[3], (SEQS, DOC_LEN, D), 3.0, 18.0, ((0, 8), (1, 4)))
    norm_gain = jnp.clip(1.0 + 0.1 * jax.random.normal(splits[4], (D,), jnp.float32), 0.5, 1.5)
    expert_ids_keys = jax.random.split(jax.random.fold_in(splits[5], 1), SEQS * DEC_DEV // DEC_DEV)
    expert_ids_turns = jax.random.permutation(jax.random.fold_in(splits[5], 3), SEQS * DEC_DEV // DEC_DEV)
    expert_ids = jax.vmap(lambda own, number: assign_block(jax.random.fold_in(splits[5], 2), own, number, DEC_DEV, EXPERTS, TOP, CAP, 2))(expert_ids_keys, expert_ids_turns).reshape((SEQS, DEC_DEV, TOP))
    gate_values = jnp.clip(0.5 + 2.0 * jax.random.uniform(splits[6], (SEQS, DEC_DEV, TOP), jnp.float32) ** steps_of(splits[6], (SEQS, DEC_DEV, TOP), ((0, 8),), -0.2, 0.2), 0.5, 2.5)
    expert_weights = bell_draw(splits[7], (EXPERTS, EXPERT_FF, 2, D), D ** -0.5, 0.125, ((0, 8), (1, 4)))
    return dict(states=states, out_grad=out_grad, doc_keys=doc_keys, doc_values=doc_values, norm_gain=norm_gain, expert_ids=expert_ids, gate_values=gate_values, expert_weights=expert_weights)


EPSILON = 1e-05

def attend_back(items):
    normed, doc_keys, doc_values, upstream = items
    scale = HEAD ** (-0.5)
    queries = normed.reshape(DEC_DEV, HEADS, HEAD).astype(jnp.float32)
    key_heads = doc_keys.reshape(DOC_LEN, HEADS, HEAD).astype(jnp.float32)
    value_heads = doc_values.reshape(DOC_LEN, HEADS, HEAD).astype(jnp.float32)
    grad_heads = upstream.reshape(DEC_DEV, HEADS, HEAD).astype(jnp.float32)
    highest = lax.Precision.HIGHEST
    scores = jnp.einsum('qhd,khd->hqk', queries, key_heads, precision=highest) * scale
    peak = lax.optimization_barrier(jnp.max(scores, axis=-1, keepdims=True))
    weights = jnp.exp(scores - peak)
    probs = weights / lax.optimization_barrier(jnp.sum(weights, axis=-1, keepdims=True))
    slopes = jnp.einsum('qhd,khd->hqk', grad_heads, value_heads, precision=highest)
    delta = lax.optimization_barrier(jnp.sum(probs * slopes, axis=-1, keepdims=True))
    score_grad = (probs * (slopes - delta)).astype(jnp.bfloat16).astype(jnp.float32)
    probs_low = probs.astype(jnp.bfloat16).astype(jnp.float32)
    values_grad = jnp.einsum('hqk,qhd->khd', probs_low, grad_heads, precision=highest)
    keys_grad = jnp.einsum('hqk,qhd->khd', score_grad, queries, precision=highest) * scale
    query_grad = jnp.einsum('hqk,khd->qhd', score_grad, key_heads, precision=highest) * scale
    return (query_grad.reshape(DEC_DEV, D), keys_grad.reshape(DOC_LEN, D).astype(jnp.bfloat16), values_grad.reshape(DOC_LEN, D).astype(jnp.bfloat16))

def expert_back(normed, out_grad, expert_ids, gate_values, expert_weights):
    assigned = SEQS * DEC_DEV * TOP
    slot_total = SEQS * CAP
    group_width = EXPERT_FF // N_CTX
    flat_ids = expert_ids.reshape(assigned)
    gate_flat = gate_values.reshape(assigned).astype(jnp.float32)
    rows_all = normed.reshape(SEQS * DEC_DEV, D)
    grads_all = out_grad.reshape(SEQS * DEC_DEV, D)

    def step(carry, item):
        index, weights = item
        found = jnp.nonzero(flat_ids == index, size=slot_total, fill_value=assigned)[0].astype(jnp.int32)
        filled = found < assigned
        safe_index = jnp.minimum(found, assigned - 1)
        source = safe_index // TOP
        rows = jnp.where(filled[:, None], rows_all[source], jnp.zeros((), rows_all.dtype))
        gates = jnp.where(filled, gate_flat[safe_index], 0.0)
        douts = (gates[:, None] * grads_all[source].astype(jnp.float32)).astype(jnp.bfloat16)
        w_in = weights[:, 0, :]
        w_out = weights[:, 1, :]
        pre = jnp.dot(rows, w_in.T, preferred_element_type=jnp.float32)
        act, pull = jax.vjp(jax.nn.gelu, pre)
        act_low = act.astype(jnp.bfloat16)
        act_grad = jnp.dot(douts, w_out.T, preferred_element_type=jnp.float32)
        pre_grad = pull(act_grad)[0].astype(jnp.bfloat16)
        grad_in = jnp.dot(pre_grad.T, rows, preferred_element_type=jnp.float32)
        grad_out = jnp.dot(act_low.T, douts, preferred_element_type=jnp.float32)
        stacked = jnp.stack([grad_in, grad_out], axis=1).astype(jnp.bfloat16)
        pieces = jnp.einsum('sch,chd->scd', pre_grad.reshape(slot_total, N_CTX, group_width).astype(jnp.float32), w_in.reshape(N_CTX, group_width, D).astype(jnp.float32), precision=lax.Precision.HIGHEST)
        summed = lax.optimization_barrier(jnp.sum(pieces.astype(jnp.bfloat16).astype(jnp.float32), axis=1))
        carry = carry.at[source].add(jnp.where(filled[:, None], summed, 0.0))
        return (carry, stacked)
    start = jnp.zeros((SEQS * DEC_DEV, D), jnp.float32)
    moe_grad, weights_grad = lax.scan(step, start, (jnp.arange(EXPERTS, dtype=jnp.int32), expert_weights))
    return (moe_grad, weights_grad)

def reference(states, out_grad, doc_keys, doc_values, norm_gain, expert_ids, gate_values, expert_weights):
    inputs = states.astype(jnp.float32)
    inverse = lax.rsqrt(lax.optimization_barrier(jnp.mean(inputs * inputs, axis=-1, keepdims=True)) + EPSILON)
    unit = inputs * inverse
    normed = (unit * norm_gain).astype(jnp.bfloat16)
    query_grad, keys_grad, values_grad = lax.map(attend_back, (normed, doc_keys, doc_values, out_grad))
    moe_grad, weights_grad = expert_back(normed, out_grad, expert_ids, gate_values, expert_weights)
    total_grad = query_grad + moe_grad.reshape(SEQS, DEC_DEV, D)
    scaled = total_grad * norm_gain
    states_grad = out_grad.astype(jnp.float32) + inverse * (scaled - unit * lax.optimization_barrier(jnp.mean(scaled * unit, axis=-1, keepdims=True)))
    return (states_grad.astype(jnp.bfloat16), keys_grad, values_grad, weights_grad)
```

```python
import functools
import math
import jax
import jax.numpy as jnp
from jax import lax
from jax.experimental import pallas as pl
from jax.experimental.pallas import tpu as pltpu
from jax.sharding import PartitionSpec as P

HEADS = 20
HEAD = 128
TOP = 2


EPSILON = 1e-05
MESH = pl.DeviceIdType.MESH
F32 = jnp.float32
BF16 = jnp.bfloat16
VMEM_LIMIT = 60 * 1024 * 1024


def dot(a, b, ca, cb):
    return lax.dot_general(a, b, (((ca,), (cb,)), ((), ())), preferred_element_type=F32)


def head_cols(h):
    return pl.ds(pl.multiple_of(h * HEAD, HEAD), HEAD)


def gelu_pair(v):
    slope, cubic = math.sqrt(2.0 / math.pi), 0.044715
    square = v * v
    tanh = jnp.tanh(slope * v * (1.0 + cubic * square))
    half = 0.5 * (1.0 + tanh)
    inner = slope * (1.0 + 3.0 * cubic * square)
    return v * half, half + 0.5 * v * (1.0 - tanh * tanh) * inner


def block_kernel(
    ctx_count, experts, order, groups,
    states, upstream, gain, ids, gates, keys_hbm, values_hbm, weights_hbm,
    rows_out, pre_grad_out, activ_out, keys_grad_out, values_grad_out, states_grad,
    keys, values, weights, w_in, w_out, base, slots, gate_rows, outgoing, to_partner,
    got, rows, pre_grad, activ, partial, from_partner, select, select_near, query, local_total,
    stats, stats_all, merged, keys_grad, values_grad,
    parts, reduced, returned, local_parts, finals, total,
    load_sem, store_sem, direct_sem, partner_sem, full_sem, half_sem, stats_sem,
    near_sem, part_sem, back_sem, local_sem, final_sem,
):
    c, e = lax.axis_index("ctx"), lax.axis_index("exp")
    chips = experts // 2
    tokens, model_width = states.shape
    capacity = got.shape[3]
    hidden = w_in.shape[0]
    pair = 2 * capacity
    width = finals.shape[2]
    tiles = model_width // HEAD
    row_count = ctx_count // 2
    sets = row_count // 2
    x, y = lax.rem(c, 2), c // 2
    z, k = e // 2, lax.rem(e, 2)
    remote = range(1, chips)
    x_peer, partner = y * 2 + (1 - x), z * 2 + (1 - k)
    near_core, far_core = lax.rem(k + y, 2), lax.rem(k + 1 + y, 2)

    def chip_at(offset):
        return lax.rem(z + offset + chips, chips)

    def row_peer(d):
        return lax.rem(y + d, row_count) * 2 + x

    def if_carrier(p, run, other=None):
        if sets == 1:
            run()
        else:
            carrier = y // 2 == p % sets
            pl.when(carrier)(run)
            if other is not None:
                pl.when(jnp.logical_not(carrier))(other)

    def remote_copy(src, dst, sem, at, to_c, to_e, got_at=None):
        return pltpu.make_async_remote_copy(
            src_ref=src, dst_ref=dst,
            send_sem=sem.at[(0, *at)], recv_sem=sem.at[(1, *(at if got_at is None else got_at))],
            device_id={"ctx": to_c, "exp": to_e}, device_id_type=MESH,
        )

    load_keys = pltpu.make_async_copy(keys_hbm, keys, load_sem.at[0])
    load_values = pltpu.make_async_copy(values_hbm, values, load_sem.at[1])
    load_weights = pltpu.make_async_copy(weights_hbm, weights, load_sem.at[2])
    load_keys.start()
    load_values.start()
    load_weights.start()

    barrier = pltpu.get_barrier_semaphore()
    for d in range(1, ctx_count):
        pl.semaphore_signal(barrier, inc=1, device_id={"ctx": lax.rem(c + d, ctx_count), "exp": e}, device_id_type=MESH)
    for d in range(1, experts):
        pl.semaphore_signal(barrier, inc=1, device_id={"ctx": c, "exp": lax.rem(e + d, experts)}, device_id_type=MESH)

    def direct_copy(p):
        to = chip_at(-order[p]) * 2 + near_core
        return remote_copy(outgoing.at[p - 1], got.at[x, p, k], direct_sem, (p,), c, to)

    def direct_arrived(p):
        landed = got.at[x, p, near_core]
        return remote_copy(landed, landed, direct_sem, (p,), c, partner)

    def partner_copy(t):
        return remote_copy(to_partner.at[t], got.at[t, 0, k], partner_sem, (t,), c, partner)

    def partner_arrived(t):
        landed = got.at[t, 0, 1 - k]
        return remote_copy(landed, landed, partner_sem, (t,), c, partner)

    def full_x_copy(p):
        block = got.at[x, p, near_core]
        return remote_copy(block, block, full_sem, (p, 0), x_peer, e)

    def full_y_copy(p, d):
        block = got.at[x, p, near_core]
        return remote_copy(block, block, full_sem, (p, d), row_peer(d), e, (p, 2 - d % 2))

    def full_block(p, way):
        return (got.at[1 - x, p, near_core], got.at[x, p, far_core], got.at[x, p, near_core])[way]

    def full_arrived(p, way):
        landed = full_block(p, way)
        return remote_copy(landed, landed, full_sem, (p, way), c, partner)

    middle = (tiles // 2) * HEAD
    halves = (pl.ds(0, middle), pl.ds(middle, model_width - middle))

    def half_y_copy(p, d):
        block = got.at[1 - x, p, near_core].at[:, halves[0]]
        return remote_copy(block, block, half_sem, (p, d + 1), row_peer(d), e, (p, 1 - d % 2))

    def half_x_copy(p, even):
        block = full_block(p, 1 + even).at[:, halves[1]]
        return remote_copy(block, block, half_sem, (p, even), x_peer, e, (p, 2 + even))

    def half_arrived(p, way, even):
        landed = got.at[1 - x, p, (far_core, near_core)[even]].at[:, halves[way]]
        return remote_copy(landed, landed, half_sem, (p, way * 2 + even), c, partner)

    def stats_copy(d):
        return remote_copy(
            stats, stats_all.at[ctx_count - 1 - d], stats_sem, (d - 1,), lax.rem(c + d, ctx_count), e
        )

    def stats_arrived(d):
        landed = stats_all.at[ctx_count - 1 - d]
        return remote_copy(landed, landed, stats_sem, (d - 1,), c, partner)

    inputs = states[...].astype(F32)
    inverse = lax.rsqrt(jnp.mean(inputs * inputs, axis=-1, keepdims=True) + EPSILON)
    base[0] = (inputs * inverse * gain[...][None]).astype(BF16)
    base[1] = upstream[...]
    normed = base.at[0]
    expert = lax.broadcasted_iota(jnp.int32, (experts, tokens), 0)
    first, second = ids[0:1, :] == expert, ids[1:2, :] == expert
    chosen = jnp.where(first | second, 1.0, 0.0)
    gate_rows[...] = jnp.where(first, gates[0:1, :], jnp.where(second, gates[1:2, :], 0.0))
    before = jnp.where(
        lax.broadcasted_iota(jnp.int32, (tokens, tokens), 0) < lax.broadcasted_iota(jnp.int32, (tokens, tokens), 1),
        1.0, 0.0,
    ).astype(BF16)
    slots[...] = jnp.where(chosen > 0.5, dot(chosen.astype(BF16), before, 1, 0), -float(4 * tokens))

    def picked(expert_at, count, start):
        number = lax.broadcasted_iota(jnp.int32, (count, tokens), 0) - start
        return jnp.where(slots[pl.ds(expert_at, 1), :] == number.astype(F32), 1.0, 0.0)

    def gathered(expert_at, t):
        chosen_rows = picked(expert_at, capacity, 0)
        gate = jnp.sum(chosen_rows * gate_rows[pl.ds(expert_at, 1), :], axis=1, keepdims=True)
        scale = jnp.where(t == 0, 1.0, gate)
        return (dot(chosen_rows.astype(BF16), base[t], 1, 0) * scale).astype(BF16)

    pl.semaphore_wait(barrier, ctx_count + experts - 2)
    for p in remote:
        def run():
            outgoing[p - 1] = gathered(chip_at(-order[p]) * 2 + near_core, x)
            direct_copy(p).start()

        if_carrier(p, run)
    for t in range(2):
        to_partner[t] = gathered(partner, t)
        partner_copy(t).start()

    load_keys.wait()
    load_values.wait()

    def first_pass(h, carry):
        cols = head_cols(h)
        scores = dot(keys[:, cols], normed[:, cols], 1, 1) * HEAD ** (-0.5)
        peak = jnp.max(scores, axis=0, keepdims=True)
        weight = jnp.exp(scores - peak)
        slopes = dot(values[:, cols], upstream[:, cols], 1, 1)
        stats[0, pl.ds(h, 1), :] = peak
        stats[1, pl.ds(h, 1), :] = jnp.sum(weight, axis=0, keepdims=True)
        stats[2, pl.ds(h, 1), :] = jnp.sum(weight * slopes, axis=0, keepdims=True)
        return carry

    lax.fori_loop(0, HEADS, first_pass, 0, unroll=4)
    for d in range(1, ctx_count):
        stats_copy(d).start()
    for t in range(2):
        got[t, 0, k] = gathered(e, t)

    chunk = 32
    load_weights.wait()

    def split(i, carry):
        at = pl.ds(pl.multiple_of(i * chunk, chunk), chunk)
        both = jnp.swapaxes(weights[at], 0, 1)
        w_in[at, :] = both[0]
        w_out[at, :] = both[1]
        return carry

    lax.fori_loop(0, hidden // chunk, split, 0)

    def second_pass(h, carry):
        cols = head_cols(h)
        key, q, g = keys[:, cols], normed[:, cols], upstream[:, cols]
        scores = dot(key, q, 1, 1) * HEAD ** (-0.5)
        probs = jnp.exp(scores - merged[0, pl.ds(h, 1), :]) / merged[1, pl.ds(h, 1), :]
        slopes = dot(values[:, cols], g, 1, 1)
        score_grad = (probs * (slopes - merged[2, pl.ds(h, 1), :])).astype(BF16)
        values_grad[:, cols] = dot(probs.astype(BF16), g, 1, 0).astype(BF16)
        keys_grad[:, cols] = (dot(score_grad, q, 1, 0) * HEAD ** (-0.5)).astype(BF16)
        query[:, cols] = dot(score_grad, key, 0, 0) * HEAD ** (-0.5)
        return carry

    steps = 4
    quarter = HEADS // steps

    def attend(i):
        lax.fori_loop(i * quarter, (i + 1) * quarter, second_pass, 0, unroll=quarter)

    def merge_stats():
        for d in range(1, ctx_count):
            stats_arrived(d).wait_recv()
        peak = stats[0]
        for d in range(ctx_count - 1):
            peak = jnp.maximum(peak, stats_all[d, 0])
        factor = jnp.exp(stats[0] - peak)
        denominator, inner = stats[1] * factor, stats[2] * factor
        for d in range(ctx_count - 1):
            factor = jnp.exp(stats_all[d, 0] - peak)
            denominator = denominator + stats_all[d, 1] * factor
            inner = inner + stats_all[d, 2] * factor
        merged[0] = peak
        merged[1] = denominator
        merged[2] = inner / denominator

    def forward(p):
        def run():
            direct_arrived(p).wait_recv()
            full_x_copy(p).start()
            for d in range(1, row_count):
                full_y_copy(p, d).start()

        if_carrier(p, run)

    def forward_halves(p):
        def run():
            full_arrived(p, 0).wait_recv()
            for d in range(1, row_count):
                half_y_copy(p, d).start()

        def other():
            full_arrived(p, 2).wait_recv()
            half_x_copy(p, 1).start()

        if_carrier(p, run, other)
        full_arrived(p, 1).wait_recv()
        half_x_copy(p, 0).start()

    def halves_arrived(p):
        def other():
            for way in range(2):
                half_arrived(p, way, 1).wait_recv()

        if_carrier(p, lambda: None, other)
        for way in range(2):
            half_arrived(p, way, 0).wait_recv()

    def pack(p):
        at = pl.ds(p * pair, pair)
        for t in range(2):
            rows[t, at, :] = got[t, p].reshape(pair, model_width)
            rows_store(t, p).start()

    def rows_store(t, p):
        at = pl.ds(p * pair, pair)
        return pltpu.make_async_copy(rows.at[t, at], rows_out.at[t, at], store_sem.at[2 + t * chips + p])

    block = min(hidden, 256)
    step = HEAD * math.gcd(tiles, 5)

    def expert(group):
        at = pl.ds(group[0] * pair, len(group) * pair)
        for i in range(hidden // block):
            part = pl.ds(i * block, block)
            pre = dot(rows[0, at, :], w_in[part, :], 1, 1)
            act_grad = dot(rows[1, at, :], w_out[part, :], 1, 1)
            act, slope = gelu_pair(pre)
            activ[at, part] = act.astype(BF16)
            pre_grad[at, part] = (act_grad * slope).astype(BF16)
        for i in range(model_width // step):
            part = pl.ds(i * step, step)
            partial[at, part] = dot(pre_grad[at, :], w_in[:, part], 1, 0).astype(BF16)

    def share(owner):
        return pl.ds(pl.multiple_of(owner * tiles // ctx_count * HEAD, HEAD), width)

    def near_copy():
        return remote_copy(partial.at[pl.ds(0, pair), :], from_partner, near_sem, (0,), c, partner)

    def part_copy(p, d):
        peer = lax.rem(c + d, ctx_count)
        return remote_copy(
            partial.at[pl.ds(p * pair, pair), share(peer)], parts.at[p - 1, ctx_count - 1 - d],
            part_sem, (p, d - 1), peer, e,
        )

    def part_arrived(p, d):
        landed = parts.at[p - 1, ctx_count - 1 - d]
        return remote_copy(landed, landed, part_sem, (p, d - 1), c, partner)

    def back_position(p):
        return order.index((chips - order[p]) % chips)

    def back_copy(p, core):
        to = chip_at(order[p]) * 2 + core
        at = back_position(p)
        return pltpu.make_async_remote_copy(
            src_ref=reduced.at[p - 1, core], dst_ref=returned.at[at - 1, k],
            send_sem=back_sem.at[0, p, core], recv_sem=back_sem.at[1, at, k],
            device_id={"ctx": c, "exp": to}, device_id_type=MESH,
        )

    def back_arrived(p, core):
        landed = returned.at[p - 1, core]
        return remote_copy(landed, landed, back_sem, (p, core), c, partner)

    def local_copy(d):
        peer = lax.rem(c + d, ctx_count)
        return remote_copy(
            local_total.at[:, share(peer)], local_parts.at[ctx_count - 1 - d], local_sem, (d - 1,), peer, e
        )

    def local_arrived(d):
        landed = local_parts.at[ctx_count - 1 - d]
        return remote_copy(landed, landed, local_sem, (d - 1,), c, partner)

    def final_copy(d):
        peer = lax.rem(c + d, ctx_count)
        return remote_copy(finals.at[c], finals.at[c], final_sem, (d - 1,), peer, e)

    def final_arrived(d):
        landed = finals.at[lax.rem(c + ctx_count - d, ctx_count)]
        return remote_copy(landed, landed, final_sem, (d - 1,), c, partner)

    far_first = sorted(range(1, ctx_count), key=lambda d: d != ctx_count // 2)

    def send_parts(p):
        for d in far_first:
            part_copy(p, d).start()

    def reduce_parts(p):
        summed = partial[pl.ds(p * pair, pair), share(c)].astype(F32)
        for d in far_first:
            part_arrived(p, d).wait_recv()
        for d in range(ctx_count - 1):
            summed = summed + parts[p - 1, d].astype(F32)
        reduced[p - 1] = summed.astype(BF16).reshape(2, capacity, width)
        for core in range(2):
            back_copy(p, core).start()

    def near_total():
        near_copy().wait_recv()
        for i in range(model_width // step):
            part = pl.ds(i * step, step)
            local_total[:, part] = (
                query[:, part]
                + dot(select_near[0], partial[pl.ds(0, pair), part], 0, 0)
                + dot(select_near[1], from_partner[:, part], 0, 0)
            ).astype(BF16)
        for d in far_first:
            local_copy(d).start()

    merge_stats()
    attend(0)
    forward(1)
    attend(1)
    for p in range(2, chips):
        forward(p)
        forward_halves(p - 1)
        if p < steps:
            attend(p)
    for i in range(max(chips, 2), steps):
        attend(i)
    forward_halves(chips - 1)
    for i in range(2):
        select_near[i] = picked((e, partner)[i], pair, k * capacity).astype(BF16)
    for p in remote:
        for core in range(2):
            select[p - 1, core] = picked(chip_at(order[p]) * 2 + core, capacity, 0).astype(BF16)
    keys_store = pltpu.make_async_copy(keys_grad, keys_grad_out, store_sem.at[0])
    values_store = pltpu.make_async_copy(values_grad, values_grad_out, store_sem.at[1])
    keys_store.start()
    values_store.start()
    for t in range(2):
        partner_arrived(t).wait_recv()
    pack(0)
    for group in groups:
        for p in group:
            if p:
                halves_arrived(p)
                pack(p)
        expert(group)
        for p in group:
            if p:
                send_parts(p)
            else:
                near_copy().start()
        if group[0] == 0:
            near_total()
        else:
            for p in previous:
                if p:
                    reduce_parts(p)
        previous = group
    pre_grad_store = pltpu.make_async_copy(pre_grad, pre_grad_out, store_sem.at[2 + 2 * chips])
    activ_store = pltpu.make_async_copy(activ, activ_out, store_sem.at[3 + 2 * chips])
    pre_grad_store.start()
    activ_store.start()
    for p in previous:
        if p:
            reduce_parts(p)
    for d in far_first:
        local_arrived(d).wait_recv()
    summed = local_total[:, share(c)].astype(F32)
    for d in range(ctx_count - 1):
        summed = summed + local_parts[d].astype(F32)
    for p in sorted(remote, key=back_position):
        for core in range(2):
            back_arrived(p, core).wait_recv()
            summed = summed + dot(select[p - 1, core], returned[p - 1, core], 0, 0)
    finals[c] = summed.astype(BF16)
    for d in far_first:
        final_copy(d).start()
    for d in far_first:
        final_arrived(d).wait_recv()
    for owner in range(ctx_count):
        total[:, pl.ds(owner * tiles // ctx_count * HEAD, width)] = finals[owner]
    lines = 32

    def norm_gradient(i, carry):
        at = pl.ds(pl.multiple_of(i * lines, lines), lines)
        values_in = states[at, :].astype(F32)
        scale = lax.rsqrt(jnp.mean(values_in * values_in, axis=-1, keepdims=True) + EPSILON)
        unit = values_in * scale
        scaled = total[at, :].astype(F32) * gain[...][None]
        states_grad[at, :] = (
            upstream[at, :].astype(F32) + scale * (scaled - unit * jnp.mean(scaled * unit, axis=-1, keepdims=True))
        ).astype(BF16)
        return carry

    lax.fori_loop(0, tokens // lines, norm_gradient, 0)

    keys_store.wait()
    values_store.wait()
    pre_grad_store.wait()
    activ_store.wait()
    for t in range(2):
        partner_copy(t).wait_send()
        for p in range(chips):
            rows_store(t, p).wait()
    near_copy().wait_send()
    for d in range(1, ctx_count):
        stats_copy(d).wait_send()
        local_copy(d).wait_send()
        final_copy(d).wait_send()
    for p in remote:
        def run():
            direct_copy(p).wait_send()
            full_x_copy(p).wait_send()
            for d in range(1, row_count):
                full_y_copy(p, d).wait_send()
                half_y_copy(p, d).wait_send()

        if_carrier(p, run, lambda: half_x_copy(p, 1).wait_send())
        half_x_copy(p, 0).wait_send()
        for core in range(2):
            back_copy(p, core).wait_send()
        for d in range(1, ctx_count):
            part_copy(p, d).wait_send()


def weights_kernel(pre_grad, activ, rows, grad):
    both = jnp.stack([
        dot(pre_grad[...], rows[0], 0, 0).astype(BF16),
        dot(activ[...], rows[1], 0, 0).astype(BF16),
    ])
    grad[...] = jnp.swapaxes(both, 0, 1)


def on_device(
    states, out_grad, doc_keys, doc_values, norm_gain, expert_ids, gate_values, expert_weights
):
    tokens, model_width = states.shape[1:]
    key_count = doc_keys.shape[1]
    ctx_count, experts = lax.axis_size("ctx"), lax.axis_size("exp")
    chips = experts // 2
    hidden = expert_weights.shape[1]
    capacity = 8 * -(-5 * TOP * tokens // (32 * experts))
    pair = 2 * capacity
    slot_rows = experts * capacity
    tiles = model_width // HEAD
    width = HEAD * max(-(-(c + 1) * tiles // ctx_count) - c * tiles // ctx_count for c in range(ctx_count))
    order = [0] + sorted(range(1, chips), key=lambda j: abs(j - chips // 2))
    groups = [[0, 1]] + [[p] for p in range(2, chips)]
    vmem = pl.BlockSpec(memory_space=pltpu.VMEM)
    anywhere = pl.BlockSpec(memory_space=pl.ANY)
    shape = jax.ShapeDtypeStruct
    dma = pltpu.SemaphoreType.DMA
    near = max(chips - 1, 1)
    scratch = [
        ((key_count, model_width), BF16),
        ((key_count, model_width), BF16),
        ((hidden, 2, model_width), BF16),
        ((hidden, model_width), BF16),
        ((hidden, model_width), BF16),
        ((2, tokens, model_width), BF16),
        ((experts, tokens), F32),
        ((experts, tokens), F32),
        ((near, capacity, model_width), BF16),
        ((2, capacity, model_width), BF16),
        ((2, chips, 2, capacity, model_width), BF16),
        ((2, slot_rows, model_width), BF16),
        ((slot_rows, hidden), BF16),
        ((slot_rows, hidden), BF16),
        ((slot_rows, model_width), BF16),
        ((pair, model_width), BF16),
        ((near, 2, capacity, tokens), BF16),
        ((2, pair, tokens), BF16),
        ((tokens, model_width), F32),
        ((tokens, model_width), BF16),
        ((3, HEADS, tokens), F32),
        ((ctx_count - 1, 3, HEADS, tokens), F32),
        ((3, HEADS, tokens), F32),
        ((key_count, model_width), BF16),
        ((key_count, model_width), BF16),
        ((near, ctx_count - 1, pair, width), BF16),
        ((near, 2, capacity, width), BF16),
        ((near, 2, capacity, width), BF16),
        ((ctx_count - 1, tokens, width), BF16),
        ((ctx_count, tokens, width), BF16),
        ((tokens, model_width), BF16),
    ]
    semaphores = [
        (3,),
        (4 + 2 * chips,),
        (2, chips),
        (2, 2),
        (2, chips, max(ctx_count // 2, 3)),
        (2, chips, max(ctx_count // 2 + 1, 4)),
        (2, ctx_count - 1),
        (2, 1),
        (2, chips, ctx_count - 1),
        (2, chips, 2),
        (2, ctx_count - 1),
        (2, ctx_count - 1),
    ]
    rows, pre_grad, activ, keys_grad, values_grad, states_grad = pl.pallas_call(
        functools.partial(block_kernel, ctx_count, experts, order, groups),
        out_shape=(
            shape((2, slot_rows, model_width), BF16),
            shape((slot_rows, hidden), BF16),
            shape((slot_rows, hidden), BF16),
            shape((key_count, model_width), BF16),
            shape((key_count, model_width), BF16),
            shape((tokens, model_width), BF16),
        ),
        in_specs=[vmem] * 5 + [anywhere] * 3,
        out_specs=(anywhere,) * 5 + (vmem,),
        scratch_shapes=[pltpu.VMEM(s, t) for s, t in scratch] + [dma(s) for s in semaphores],
        compiler_params=pltpu.CompilerParams(
            vmem_limit_bytes=VMEM_LIMIT, collective_id=0, has_side_effects=True
        ),
    )(
        states[0], out_grad[0], norm_gain, expert_ids[0].T, gate_values[0].T,
        doc_keys[0], doc_values[0], expert_weights[0],
    )
    block = min(hidden, 128)
    hidden_spec = pl.BlockSpec((slot_rows, block), lambda i: (0, i))
    weights_grad = pl.pallas_call(
        weights_kernel,
        grid=(hidden // block,),
        out_shape=shape((hidden, 2, model_width), BF16),
        in_specs=[
            hidden_spec, hidden_spec,
            pl.BlockSpec((2, slot_rows, model_width), lambda i: (0, 0, 0)),
        ],
        out_specs=pl.BlockSpec((block, 2, model_width), lambda i: (i, 0, 0)),
        compiler_params=pltpu.CompilerParams(vmem_limit_bytes=VMEM_LIMIT),
    )(pre_grad, activ, rows)
    return states_grad[None], keys_grad[None], values_grad[None], weights_grad[None]


def solution(mesh):
    return jax.shard_map(
        on_device,
        mesh=mesh,
        in_specs=(
            P("exp", None, None),
            P("exp", None, None),
            P("exp", "ctx", None),
            P("exp", "ctx", None),
            P(),
            P("exp", None, None),
            P("exp", None, None),
            P("exp", "ctx", None, None),
        ),
        out_specs=(
            P("exp", None, None),
            P("exp", "ctx", None),
            P("exp", "ctx", None),
            P("exp", "ctx", None, None),
        ),
        check_vma=False,
    )
```

```python
import functools
import math
import jax
import jax.numpy as jnp
from jax import lax
from jax.experimental import pallas as pl
from jax.experimental.pallas import tpu as pltpu
from jax.sharding import PartitionSpec as P

HEADS = 20
HEAD = 128
TOP = 2


EPSILON = 1e-05
MESH = pl.DeviceIdType.MESH
F32 = jnp.float32
BF16 = jnp.bfloat16
VMEM_LIMIT = 60 * 1024 * 1024


def dot(a, b, ca, cb):
    return lax.dot_general(a, b, (((ca,), (cb,)), ((), ())), preferred_element_type=F32)


def head_cols(h):
    return pl.ds(pl.multiple_of(h * HEAD, HEAD), HEAD)


def gelu_pair(v):
    slope, cubic = math.sqrt(2.0 / math.pi), 0.044715
    square = v * v
    tanh = jnp.tanh(slope * v * (1.0 + cubic * square))
    half = 0.5 * (1.0 + tanh)
    inner = slope * (1.0 + 3.0 * cubic * square)
    return v * half, half + 0.5 * v * (1.0 - tanh * tanh) * inner


def block_kernel(
    ctx_count, experts, order, groups, pieces,
    states, upstream, gain, ids, gates, keys_hbm, values_hbm, weights_hbm,
    rows_out, pre_grad_out, activ_out, keys_grad_out, values_grad_out, states_grad,
    keys, values, weights, w_in, w_out, base, slots, gate_rows, outgoing, to_partner,
    got, rows, pre_grad, activ, partial, from_partner, select, select_near, query, local_total,
    stats, stats_all, merged, keys_grad, values_grad,
    parts, reduced, returned, local_parts, finals, total,
    load_sem, store_sem, direct_sem, partner_sem, full_sem, second_sem, stats_sem,
    near_sem, part_sem, back_sem, local_sem, final_sem,
):
    c, e = lax.axis_index("ctx"), lax.axis_index("exp")
    chips = experts // 2
    tokens, model_width = states.shape
    capacity = got.shape[3]
    hidden = w_in.shape[0]
    pair = 2 * capacity
    width = finals.shape[2]
    tiles = model_width // HEAD
    row_count = ctx_count // 2
    sets = row_count // 2
    x, y = lax.rem(c, 2), c // 2
    z, k = e // 2, lax.rem(e, 2)
    remote = range(1, chips)
    x_peer, partner = y * 2 + (1 - x), z * 2 + (1 - k)
    near_core, far_core = lax.rem(k + y, 2), lax.rem(k + 1 + y, 2)

    def chip_at(offset):
        return lax.rem(z + offset + chips, chips)

    def row_peer(d):
        return lax.rem(y + d, row_count) * 2 + x

    def if_carrier(p, run, other=None):
        if sets == 1:
            run()
        else:
            carrier = y // 2 == p % sets
            pl.when(carrier)(run)
            if other is not None:
                pl.when(jnp.logical_not(carrier))(other)

    def remote_copy(src, dst, sem, at, to_c, to_e, got_at=None):
        return pltpu.make_async_remote_copy(
            src_ref=src, dst_ref=dst,
            send_sem=sem.at[(0, *at)], recv_sem=sem.at[(1, *(at if got_at is None else got_at))],
            device_id={"ctx": to_c, "exp": to_e}, device_id_type=MESH,
        )

    load_keys = pltpu.make_async_copy(keys_hbm, keys, load_sem.at[0])
    load_values = pltpu.make_async_copy(values_hbm, values, load_sem.at[1])
    load_weights = pltpu.make_async_copy(weights_hbm, weights, load_sem.at[2])
    load_keys.start()
    load_values.start()
    load_weights.start()

    barrier = pltpu.get_barrier_semaphore()
    for d in range(1, ctx_count):
        pl.semaphore_signal(barrier, inc=1, device_id={"ctx": lax.rem(c + d, ctx_count), "exp": e}, device_id_type=MESH)
    for d in range(1, experts):
        pl.semaphore_signal(barrier, inc=1, device_id={"ctx": c, "exp": lax.rem(e + d, experts)}, device_id_type=MESH)

    def piece(q):
        start, end = (at * tiles // pieces * HEAD for at in (q, q + 1))
        return pl.ds(start, end - start)

    def direct_copy(p, q):
        to = chip_at(-order[p]) * 2 + near_core
        return remote_copy(
            outgoing.at[p - 1, :, piece(q)], got.at[x, p, k].at[:, piece(q)], direct_sem, (p, q), c, to
        )

    def direct_arrived(p, q):
        landed = got.at[x, p, near_core].at[:, piece(q)]
        return remote_copy(landed, landed, direct_sem, (p, q), c, partner)

    def partner_copy(t):
        return remote_copy(to_partner.at[t], got.at[t, 0, k], partner_sem, (t,), c, partner)

    def partner_arrived(t):
        landed = got.at[t, 0, 1 - k]
        return remote_copy(landed, landed, partner_sem, (t,), c, partner)

    def full_x_copy(p, q):
        block = got.at[x, p, near_core].at[:, piece(q)]
        return remote_copy(block, block, full_sem, (p, 0, q), x_peer, e)

    def full_y_copy(p, d, q):
        block = got.at[x, p, near_core].at[:, piece(q)]
        return remote_copy(block, block, full_sem, (p, d, q), row_peer(d), e, (p, 2 - d % 2, q))

    def full_block(p, way, q):
        block = (got.at[1 - x, p, near_core], got.at[x, p, far_core], got.at[x, p, near_core])[way]
        return block.at[:, piece(q)]

    def full_arrived(p, way, q):
        landed = full_block(p, way, q)
        return remote_copy(landed, landed, full_sem, (p, way, q), c, partner)

    def second_y_copy(p, d, q):
        block = got.at[1 - x, p, near_core].at[:, piece(q)]
        return remote_copy(block, block, second_sem, (p, d + 1, q), row_peer(d), e, (p, 1 - d % 2, q))

    def second_x_copy(p, even, q):
        block = full_block(p, 1 + even, q)
        return remote_copy(block, block, second_sem, (p, even, q), x_peer, e)

    def second_arrived(p, even, q):
        landed = got.at[1 - x, p, (far_core, near_core)[even]].at[:, piece(q)]
        return remote_copy(landed, landed, second_sem, (p, even, q), c, partner)

    def stats_copy(d):
        return remote_copy(
            stats, stats_all.at[ctx_count - 1 - d], stats_sem, (d - 1,), lax.rem(c + d, ctx_count), e
        )

    def stats_arrived(d):
        landed = stats_all.at[ctx_count - 1 - d]
        return remote_copy(landed, landed, stats_sem, (d - 1,), c, partner)

    inputs = states[...].astype(F32)
    inverse = lax.rsqrt(jnp.mean(inputs * inputs, axis=-1, keepdims=True) + EPSILON)
    base[0] = (inputs * inverse * gain[...][None]).astype(BF16)
    base[1] = upstream[...]
    normed = base.at[0]
    expert = lax.broadcasted_iota(jnp.int32, (experts, tokens), 0)
    first, second = ids[0:1, :] == expert, ids[1:2, :] == expert
    chosen = jnp.where(first | second, 1.0, 0.0)
    gate_rows[...] = jnp.where(first, gates[0:1, :], jnp.where(second, gates[1:2, :], 0.0))
    before = jnp.where(
        lax.broadcasted_iota(jnp.int32, (tokens, tokens), 0) < lax.broadcasted_iota(jnp.int32, (tokens, tokens), 1),
        1.0, 0.0,
    ).astype(BF16)
    slots[...] = jnp.where(chosen > 0.5, dot(chosen.astype(BF16), before, 1, 0), -float(4 * tokens))

    def picked(expert_at, count, start):
        number = lax.broadcasted_iota(jnp.int32, (count, tokens), 0) - start
        return jnp.where(slots[pl.ds(expert_at, 1), :] == number.astype(F32), 1.0, 0.0)

    def gathered(expert_at, t, cols):
        chosen_rows = picked(expert_at, capacity, 0)
        gate = jnp.sum(chosen_rows * gate_rows[pl.ds(expert_at, 1), :], axis=1, keepdims=True)
        scale = jnp.where(t == 0, 1.0, gate)
        return (dot(chosen_rows.astype(BF16), base[t, :, cols], 1, 0) * scale).astype(BF16)

    pl.semaphore_wait(barrier, ctx_count + experts - 2)
    for p in remote:
        def run():
            for q in range(pieces):
                outgoing[p - 1, :, piece(q)] = gathered(chip_at(-order[p]) * 2 + near_core, x, piece(q))
                direct_copy(p, q).start()

        if_carrier(p, run)
    for t in range(2):
        to_partner[t] = gathered(partner, t, slice(None))
        partner_copy(t).start()

    load_keys.wait()
    load_values.wait()

    def first_pass(h, carry):
        cols = head_cols(h)
        scores = dot(keys[:, cols], normed[:, cols], 1, 1) * HEAD ** (-0.5)
        peak = jnp.max(scores, axis=0, keepdims=True)
        weight = jnp.exp(scores - peak)
        slopes = dot(values[:, cols], upstream[:, cols], 1, 1)
        stats[0, pl.ds(h, 1), :] = peak
        stats[1, pl.ds(h, 1), :] = jnp.sum(weight, axis=0, keepdims=True)
        stats[2, pl.ds(h, 1), :] = jnp.sum(weight * slopes, axis=0, keepdims=True)
        return carry

    lax.fori_loop(0, HEADS, first_pass, 0, unroll=4)
    for d in range(1, ctx_count):
        stats_copy(d).start()
    for t in range(2):
        got[t, 0, k] = gathered(e, t, slice(None))

    chunk = 32

    def split(i, carry):
        at = pl.ds(pl.multiple_of(i * chunk, chunk), chunk)
        both = jnp.swapaxes(weights[at], 0, 1)
        w_in[at, :] = both[0]
        w_out[at, :] = both[1]
        return carry

    def second_pass(h, carry):
        cols = head_cols(h)
        key, q, g = keys[:, cols], normed[:, cols], upstream[:, cols]
        scores = dot(key, q, 1, 1) * HEAD ** (-0.5)
        probs = jnp.exp(scores - merged[0, pl.ds(h, 1), :]) / merged[1, pl.ds(h, 1), :]
        slopes = dot(values[:, cols], g, 1, 1)
        score_grad = (probs * (slopes - merged[2, pl.ds(h, 1), :])).astype(BF16)
        values_grad[:, cols] = dot(probs.astype(BF16), g, 1, 0).astype(BF16)
        keys_grad[:, cols] = (dot(score_grad, q, 1, 0) * HEAD ** (-0.5)).astype(BF16)
        query[:, cols] = dot(score_grad, key, 0, 0) * HEAD ** (-0.5)
        return carry

    steps = 4
    quarter = HEADS // steps

    def attend(i):
        lax.fori_loop(i * quarter, (i + 1) * quarter, second_pass, 0, unroll=quarter)

    def merge_stats():
        for d in range(1, ctx_count):
            stats_arrived(d).wait_recv()
        peak = stats[0]
        for d in range(ctx_count - 1):
            peak = jnp.maximum(peak, stats_all[d, 0])
        factor = jnp.exp(stats[0] - peak)
        denominator, inner = stats[1] * factor, stats[2] * factor
        for d in range(ctx_count - 1):
            factor = jnp.exp(stats_all[d, 0] - peak)
            denominator = denominator + stats_all[d, 1] * factor
            inner = inner + stats_all[d, 2] * factor
        merged[0] = peak
        merged[1] = denominator
        merged[2] = inner / denominator

    def forward(p, q):
        def run():
            direct_arrived(p, q).wait_recv()
            if q % 2 == 0:
                full_x_copy(p, q).start()
            for d in range(1, row_count):
                full_y_copy(p, d, q).start()
            if q % 2:
                full_x_copy(p, q).start()

        if_carrier(p, run)

    def forward_again(p, q):
        def run():
            full_arrived(p, 0, q).wait_recv()
            for d in range(1, row_count):
                second_y_copy(p, d, q).start()

        def other():
            full_arrived(p, 2, q).wait_recv()
            second_x_copy(p, 1, q).start()

        if q % 2 == 0:
            if_carrier(p, run)
        else:
            if_carrier(p, lambda: None, other)
            full_arrived(p, 1, q).wait_recv()
            second_x_copy(p, 0, q).start()

    def all_arrived(p):
        for q in range(pieces):
            def run():
                if q % 2:
                    full_arrived(p, 0, q).wait_recv()

            def other():
                if q % 2 == 0:
                    full_arrived(p, 2, q).wait_recv()
                second_arrived(p, 1, q).wait_recv()

            if_carrier(p, run, other)
            if q % 2 == 0:
                full_arrived(p, 1, q).wait_recv()
            second_arrived(p, 0, q).wait_recv()

    def pack(p):
        at = pl.ds(p * pair, pair)
        for t in range(2):
            rows[t, at, :] = got[t, p].reshape(pair, model_width)
            rows_store(t, p).start()

    def rows_store(t, p):
        at = pl.ds(p * pair, pair)
        return pltpu.make_async_copy(rows.at[t, at], rows_out.at[t, at], store_sem.at[2 + t * chips + p])

    block = min(hidden, 256)
    step = HEAD * math.gcd(tiles, 5)

    def expert(group):
        at = pl.ds(group[0] * pair, len(group) * pair)
        for i in range(hidden // block):
            part = pl.ds(i * block, block)
            pre = dot(rows[0, at, :], w_in[part, :], 1, 1)
            act_grad = dot(rows[1, at, :], w_out[part, :], 1, 1)
            act, slope = gelu_pair(pre)
            activ[at, part] = act.astype(BF16)
            pre_grad[at, part] = (act_grad * slope).astype(BF16)
        for i in range(model_width // step):
            part = pl.ds(i * step, step)
            partial[at, part] = dot(pre_grad[at, :], w_in[:, part], 1, 0).astype(BF16)

    def share(owner):
        return pl.ds(pl.multiple_of(owner * tiles // ctx_count * HEAD, HEAD), width)

    def near_copy():
        return remote_copy(partial.at[pl.ds(0, pair), :], from_partner, near_sem, (0,), c, partner)

    def part_copy(p, d):
        peer = lax.rem(c + d, ctx_count)
        return remote_copy(
            partial.at[pl.ds(p * pair, pair), share(peer)], parts.at[p - 1, ctx_count - 1 - d],
            part_sem, (p, d - 1), peer, e,
        )

    def part_arrived(p, d):
        landed = parts.at[p - 1, ctx_count - 1 - d]
        return remote_copy(landed, landed, part_sem, (p, d - 1), c, partner)

    def back_position(p):
        return order.index((chips - order[p]) % chips)

    def back_copy(p, core):
        to = chip_at(order[p]) * 2 + core
        at = back_position(p)
        return pltpu.make_async_remote_copy(
            src_ref=reduced.at[p - 1, core], dst_ref=returned.at[at - 1, k],
            send_sem=back_sem.at[0, p, core], recv_sem=back_sem.at[1, at, k],
            device_id={"ctx": c, "exp": to}, device_id_type=MESH,
        )

    def back_arrived(p, core):
        landed = returned.at[p - 1, core]
        return remote_copy(landed, landed, back_sem, (p, core), c, partner)

    def local_copy(d):
        peer = lax.rem(c + d, ctx_count)
        return remote_copy(
            local_total.at[:, share(peer)], local_parts.at[ctx_count - 1 - d], local_sem, (d - 1,), peer, e
        )

    def local_arrived(d):
        landed = local_parts.at[ctx_count - 1 - d]
        return remote_copy(landed, landed, local_sem, (d - 1,), c, partner)

    def final_copy(d):
        peer = lax.rem(c + d, ctx_count)
        return remote_copy(finals.at[c], finals.at[c], final_sem, (d - 1,), peer, e)

    def final_arrived(d):
        landed = finals.at[lax.rem(c + ctx_count - d, ctx_count)]
        return remote_copy(landed, landed, final_sem, (d - 1,), c, partner)

    far_first = sorted(range(1, ctx_count), key=lambda d: d != ctx_count // 2)

    def send_parts(p):
        for d in far_first:
            part_copy(p, d).start()

    def reduce_parts(p):
        summed = partial[pl.ds(p * pair, pair), share(c)].astype(F32)
        for d in far_first:
            part_arrived(p, d).wait_recv()
        for d in range(ctx_count - 1):
            summed = summed + parts[p - 1, d].astype(F32)
        reduced[p - 1] = summed.astype(BF16).reshape(2, capacity, width)
        for core in range(2):
            back_copy(p, core).start()

    def near_total():
        near_copy().wait_recv()
        for i in range(model_width // step):
            part = pl.ds(i * step, step)
            local_total[:, part] = (
                query[:, part]
                + dot(select_near[0], partial[pl.ds(0, pair), part], 0, 0)
                + dot(select_near[1], from_partner[:, part], 0, 0)
            ).astype(BF16)

    def split_weights():
        load_weights.wait()
        lax.fori_loop(0, hidden // chunk, split, 0)

    def first_attend():
        merge_stats()
        attend(0)

    keys_store = pltpu.make_async_copy(keys_grad, keys_grad_out, store_sem.at[0])
    values_store = pltpu.make_async_copy(values_grad, values_grad_out, store_sem.at[1])

    def last_attend():
        attend(steps - 1)
        keys_store.start()
        values_store.start()
        for i in range(2):
            select_near[i] = picked((e, partner)[i], pair, k * capacity).astype(BF16)
        for p in remote:
            for core in range(2):
                select[p - 1, core] = picked(chip_at(order[p]) * 2 + core, capacity, 0).astype(BF16)
        for t in range(2):
            partner_arrived(t).wait_recv()
        pack(0)

    def run_group(group):
        for p in group:
            if p:
                all_arrived(p)
                pack(p)
        expert(group)
        for p in group:
            if p:
                send_parts(p)
            else:
                near_copy().start()
        if group[0] == 0:
            near_total()
        if group is groups[-1]:
            for d in far_first:
                local_copy(d).start()
        for p in pending:
            reduce_parts(p)
        pending[:] = [p for p in group if p]

    work = [split_weights, first_attend] + [functools.partial(attend, i) for i in range(1, steps - 1)] + [last_attend]
    pending = []
    moves = [(p, q) for p in remote for q in range(pieces)]
    lag, late = 1, 3
    for n in range(max(len(moves) + late, len(work))):
        if n < len(moves):
            forward(*moves[n])
        if n < len(work):
            work[n]()
        if 0 <= n - lag < len(moves):
            forward_again(*moves[n - lag])
        if 0 <= n - late < len(moves) and n >= len(work) - 1:
            for group in groups:
                if (group[-1], pieces - 1) == moves[n - late]:
                    run_group(group)
    pre_grad_store = pltpu.make_async_copy(pre_grad, pre_grad_out, store_sem.at[2 + 2 * chips])
    activ_store = pltpu.make_async_copy(activ, activ_out, store_sem.at[3 + 2 * chips])
    pre_grad_store.start()
    activ_store.start()
    for p in pending:
        reduce_parts(p)
    for d in far_first:
        local_arrived(d).wait_recv()
    summed = local_total[:, share(c)].astype(F32)
    for d in range(ctx_count - 1):
        summed = summed + local_parts[d].astype(F32)
    for p in sorted(remote, key=back_position):
        for core in range(2):
            back_arrived(p, core).wait_recv()
            summed = summed + dot(select[p - 1, core], returned[p - 1, core], 0, 0)
    finals[c] = summed.astype(BF16)
    for d in far_first:
        final_copy(d).start()
    for d in far_first:
        final_arrived(d).wait_recv()
    for owner in range(ctx_count):
        total[:, pl.ds(owner * tiles // ctx_count * HEAD, width)] = finals[owner]
    lines = 32

    def norm_gradient(i, carry):
        at = pl.ds(pl.multiple_of(i * lines, lines), lines)
        values_in = states[at, :].astype(F32)
        scale = lax.rsqrt(jnp.mean(values_in * values_in, axis=-1, keepdims=True) + EPSILON)
        unit = values_in * scale
        scaled = total[at, :].astype(F32) * gain[...][None]
        states_grad[at, :] = (
            upstream[at, :].astype(F32) + scale * (scaled - unit * jnp.mean(scaled * unit, axis=-1, keepdims=True))
        ).astype(BF16)
        return carry

    lax.fori_loop(0, tokens // lines, norm_gradient, 0)

    keys_store.wait()
    values_store.wait()
    pre_grad_store.wait()
    activ_store.wait()
    for t in range(2):
        partner_copy(t).wait_send()
        for p in range(chips):
            rows_store(t, p).wait()
    near_copy().wait_send()
    for d in range(1, ctx_count):
        stats_copy(d).wait_send()
        local_copy(d).wait_send()
        final_copy(d).wait_send()
    for p in remote:
        def run():
            for q in range(pieces):
                direct_copy(p, q).wait_send()
                full_x_copy(p, q).wait_send()
                for d in range(1, row_count):
                    full_y_copy(p, d, q).wait_send()
                    if q % 2 == 0:
                        second_y_copy(p, d, q).wait_send()

        def other():
            for q in range(1, pieces, 2):
                second_x_copy(p, 1, q).wait_send()

        if_carrier(p, run, other)
        for q in range(1, pieces, 2):
            second_x_copy(p, 0, q).wait_send()
        for core in range(2):
            back_copy(p, core).wait_send()
        for d in range(1, ctx_count):
            part_copy(p, d).wait_send()


def weights_kernel(pre_grad, activ, rows, grad):
    grad[:, 0, :] = dot(pre_grad[...], rows[0], 0, 0).astype(BF16)
    grad[:, 1, :] = dot(activ[...], rows[1], 0, 0).astype(BF16)


def on_device(
    states, out_grad, doc_keys, doc_values, norm_gain, expert_ids, gate_values, expert_weights
):
    tokens, model_width = states.shape[1:]
    key_count = doc_keys.shape[1]
    ctx_count, experts = lax.axis_size("ctx"), lax.axis_size("exp")
    chips = experts // 2
    hidden = expert_weights.shape[1]
    capacity = 8 * -(-5 * TOP * tokens // (32 * experts))
    pair = 2 * capacity
    slot_rows = experts * capacity
    tiles = model_width // HEAD
    width = HEAD * max(-(-(c + 1) * tiles // ctx_count) - c * tiles // ctx_count for c in range(ctx_count))
    order = [0] + sorted(range(1, chips), key=lambda j: min(j, chips - j))
    pieces = 2
    groups = [[0, 1]] + [[p] for p in range(2, chips)]
    vmem = pl.BlockSpec(memory_space=pltpu.VMEM)
    anywhere = pl.BlockSpec(memory_space=pl.ANY)
    shape = jax.ShapeDtypeStruct
    dma = pltpu.SemaphoreType.DMA
    near = max(chips - 1, 1)
    scratch = [
        ((key_count, model_width), BF16),
        ((key_count, model_width), BF16),
        ((hidden, 2, model_width), BF16),
        ((hidden, model_width), BF16),
        ((hidden, model_width), BF16),
        ((2, tokens, model_width), BF16),
        ((experts, tokens), F32),
        ((experts, tokens), F32),
        ((near, capacity, model_width), BF16),
        ((2, capacity, model_width), BF16),
        ((2, chips, 2, capacity, model_width), BF16),
        ((2, slot_rows, model_width), BF16),
        ((slot_rows, hidden), BF16),
        ((slot_rows, hidden), BF16),
        ((slot_rows, model_width), BF16),
        ((pair, model_width), BF16),
        ((near, 2, capacity, tokens), BF16),
        ((2, pair, tokens), BF16),
        ((tokens, model_width), F32),
        ((tokens, model_width), BF16),
        ((3, HEADS, tokens), F32),
        ((ctx_count - 1, 3, HEADS, tokens), F32),
        ((3, HEADS, tokens), F32),
        ((key_count, model_width), BF16),
        ((key_count, model_width), BF16),
        ((near, ctx_count - 1, pair, width), BF16),
        ((near, 2, capacity, width), BF16),
        ((near, 2, capacity, width), BF16),
        ((ctx_count - 1, tokens, width), BF16),
        ((ctx_count, tokens, width), BF16),
        ((tokens, model_width), BF16),
    ]
    semaphores = [
        (3,),
        (4 + 2 * chips,),
        (2, chips, pieces),
        (2, 2),
        (2, chips, max(ctx_count // 2, 3), pieces),
        (2, chips, ctx_count // 2 + 1, pieces),
        (2, ctx_count - 1),
        (2, 1),
        (2, chips, ctx_count - 1),
        (2, chips, 2),
        (2, ctx_count - 1),
        (2, ctx_count - 1),
    ]
    rows, pre_grad, activ, keys_grad, values_grad, states_grad = pl.pallas_call(
        functools.partial(block_kernel, ctx_count, experts, order, groups, pieces),
        out_shape=(
            shape((2, slot_rows, model_width), BF16),
            shape((slot_rows, hidden), BF16),
            shape((slot_rows, hidden), BF16),
            shape((key_count, model_width), BF16),
            shape((key_count, model_width), BF16),
            shape((tokens, model_width), BF16),
        ),
        in_specs=[vmem] * 5 + [anywhere] * 3,
        out_specs=(anywhere,) * 5 + (vmem,),
        scratch_shapes=[pltpu.VMEM(s, t) for s, t in scratch] + [dma(s) for s in semaphores],
        compiler_params=pltpu.CompilerParams(
            vmem_limit_bytes=VMEM_LIMIT, collective_id=0, has_side_effects=True
        ),
    )(
        states[0], out_grad[0], norm_gain, expert_ids[0].T, gate_values[0].T,
        doc_keys[0], doc_values[0], expert_weights[0],
    )
    block = min(hidden, 128)
    hidden_spec = pl.BlockSpec((slot_rows, block), lambda i: (0, i))
    weights_grad = pl.pallas_call(
        weights_kernel,
        grid=(hidden // block,),
        out_shape=shape((hidden, 2, model_width), BF16),
        in_specs=[
            hidden_spec, hidden_spec,
            pl.BlockSpec((2, slot_rows, model_width), lambda i: (0, 0, 0)),
        ],
        out_specs=pl.BlockSpec((block, 2, model_width), lambda i: (i, 0, 0)),
        compiler_params=pltpu.CompilerParams(vmem_limit_bytes=VMEM_LIMIT),
    )(pre_grad, activ, rows)
    return states_grad[None], keys_grad[None], values_grad[None], weights_grad[None]


def solution(mesh):
    return jax.shard_map(
        on_device,
        mesh=mesh,
        in_specs=(
            P("exp", None, None),
            P("exp", None, None),
            P("exp", "ctx", None),
            P("exp", "ctx", None),
            P(),
            P("exp", None, None),
            P("exp", None, None),
            P("exp", "ctx", None, None),
        ),
        out_specs=(
            P("exp", None, None),
            P("exp", "ctx", None),
            P("exp", "ctx", None),
            P("exp", "ctx", None, None),
        ),
        check_vma=False,
    )
```

```python
import functools
import math
import jax
import jax.numpy as jnp
from jax import lax
from jax.experimental import pallas as pl
from jax.experimental.pallas import tpu as pltpu
from jax.sharding import PartitionSpec as P

HEADS = 20
HEAD = 128
TOP = 2


EPSILON = 1e-05
MESH = pl.DeviceIdType.MESH
F32 = jnp.float32
BF16 = jnp.bfloat16
VMEM_LIMIT = 44 * 1024 * 1024
SECOND_LIMIT = 24 * 1024 * 1024


def dot(a, b, ca, cb):
    return lax.dot_general(a, b, (((ca,), (cb,)), ((), ())), preferred_element_type=F32)


def head_cols(h):
    return pl.ds(pl.multiple_of(h * HEAD, HEAD), HEAD)


def gelu_pair(v):
    slope, cubic = math.sqrt(2.0 / math.pi), 0.044715
    square = v * v
    tanh = jnp.tanh(slope * v * (1.0 + cubic * square))
    half = 0.5 * (1.0 + tanh)
    inner = slope * (1.0 + 3.0 * cubic * square)
    return v * half, half + 0.5 * v * (1.0 - tanh * tanh) * inner


def block_kernel(
    ctx_count, experts, order, groups, pieces,
    gain, ids, gates, states_hbm, upstream_hbm, keys_hbm, values_hbm, weights_hbm,
    rows, pre_grad, activ, keys_grad, values_grad, states_grad,
    states, upstream, keys, values, weights, w_in, w_out, base, slots, gate_rows, outgoing, to_partner,
    got, partial, from_partner, select, select_near, query, local_total,
    stats, stats_all, merged,
    parts, reduced, returned, local_parts, finals, total,
    load_sem, direct_sem, partner_sem, full_sem, second_sem, stats_sem,
    near_sem, part_sem, back_sem, local_sem, final_sem,
):
    c, e = lax.axis_index("ctx"), lax.axis_index("exp")
    chips = experts // 2
    tokens, model_width = states.shape
    capacity = got.shape[3]
    hidden = w_in.shape[0]
    pair = 2 * capacity
    width = finals.shape[2]
    tiles = model_width // HEAD
    row_count = ctx_count // 2
    sets = row_count // 2
    x, y = lax.rem(c, 2), c // 2
    z, k = e // 2, lax.rem(e, 2)
    remote = range(1, chips)
    x_peer, partner = y * 2 + (1 - x), z * 2 + (1 - k)
    near_core, far_core = lax.rem(k + y, 2), lax.rem(k + 1 + y, 2)

    def chip_at(offset):
        return lax.rem(z + offset + chips, chips)

    def row_peer(d):
        return lax.rem(y + d, row_count) * 2 + x

    def if_carrier(p, run, other=None):
        if sets == 1:
            run()
        else:
            carrier = y // 2 == p % sets
            pl.when(carrier)(run)
            if other is not None:
                pl.when(jnp.logical_not(carrier))(other)

    def remote_copy(src, dst, sem, at, to_c, to_e, got_at=None):
        return pltpu.make_async_remote_copy(
            src_ref=src, dst_ref=dst,
            send_sem=sem.at[(0, *at)], recv_sem=sem.at[(1, *(at if got_at is None else got_at))],
            device_id={"ctx": to_c, "exp": to_e}, device_id_type=MESH,
        )

    loads = [
        pltpu.make_async_copy(source, target, load_sem.at[n])
        for n, (source, target) in enumerate((
            (states_hbm, states), (upstream_hbm, upstream), (keys_hbm, keys),
            (values_hbm, values), (weights_hbm, weights),
        ))
    ]
    for load in loads:
        load.start()

    barrier = pltpu.get_barrier_semaphore()
    for d in range(1, ctx_count):
        pl.semaphore_signal(barrier, inc=1, device_id={"ctx": lax.rem(c + d, ctx_count), "exp": e}, device_id_type=MESH)
    for d in range(1, experts):
        pl.semaphore_signal(barrier, inc=1, device_id={"ctx": c, "exp": lax.rem(e + d, experts)}, device_id_type=MESH)

    def piece(q):
        start, end = (at * tiles // pieces * HEAD for at in (q, q + 1))
        return pl.ds(start, end - start)

    def direct_copy(p, q):
        to = chip_at(-order[p]) * 2 + near_core
        return remote_copy(
            outgoing.at[p - 1, :, piece(q)], got.at[x, p, k].at[:, piece(q)], direct_sem, (p, q), c, to
        )

    def direct_arrived(p, q):
        landed = got.at[x, p, near_core].at[:, piece(q)]
        return remote_copy(landed, landed, direct_sem, (p, q), c, partner)

    def partner_copy(t):
        return remote_copy(to_partner.at[t], got.at[t, 0, k], partner_sem, (t,), c, partner)

    def partner_arrived(t):
        landed = got.at[t, 0, 1 - k]
        return remote_copy(landed, landed, partner_sem, (t,), c, partner)

    def full_x_copy(p, q):
        block = got.at[x, p, near_core].at[:, piece(q)]
        return remote_copy(block, block, full_sem, (p, 0, q), x_peer, e)

    def full_y_copy(p, d, q):
        block = got.at[x, p, near_core].at[:, piece(q)]
        return remote_copy(block, block, full_sem, (p, d, q), row_peer(d), e, (p, 2 - d % 2, q))

    def full_block(p, way, q):
        block = (got.at[1 - x, p, near_core], got.at[x, p, far_core], got.at[x, p, near_core])[way]
        return block.at[:, piece(q)]

    def full_arrived(p, way, q):
        landed = full_block(p, way, q)
        return remote_copy(landed, landed, full_sem, (p, way, q), c, partner)

    def second_y_copy(p, d, q):
        block = got.at[1 - x, p, near_core].at[:, piece(q)]
        return remote_copy(block, block, second_sem, (p, d + 1, q), row_peer(d), e, (p, 1 - d % 2, q))

    def second_x_copy(p, even, q):
        block = full_block(p, 1 + even, q)
        return remote_copy(block, block, second_sem, (p, even, q), x_peer, e)

    def second_arrived(p, even, q):
        landed = got.at[1 - x, p, (far_core, near_core)[even]].at[:, piece(q)]
        return remote_copy(landed, landed, second_sem, (p, even, q), c, partner)

    def stats_copy(d):
        return remote_copy(
            stats, stats_all.at[ctx_count - 1 - d], stats_sem, (d - 1,), lax.rem(c + d, ctx_count), e
        )

    def stats_arrived(d):
        landed = stats_all.at[ctx_count - 1 - d]
        return remote_copy(landed, landed, stats_sem, (d - 1,), c, partner)

    loads[0].wait()
    loads[1].wait()
    inputs = states[...].astype(F32)
    inverse = lax.rsqrt(jnp.mean(inputs * inputs, axis=-1, keepdims=True) + EPSILON)
    base[0] = (inputs * inverse * gain[...][None]).astype(BF16)
    base[1] = upstream[...]
    normed = base.at[0]
    expert = lax.broadcasted_iota(jnp.int32, (experts, tokens), 0)
    first, second = ids[0:1, :] == expert, ids[1:2, :] == expert
    chosen = jnp.where(first | second, 1.0, 0.0)
    gate_rows[...] = jnp.where(first, gates[0:1, :], jnp.where(second, gates[1:2, :], 0.0))
    before = jnp.where(
        lax.broadcasted_iota(jnp.int32, (tokens, tokens), 0) < lax.broadcasted_iota(jnp.int32, (tokens, tokens), 1),
        1.0, 0.0,
    ).astype(BF16)
    slots[...] = jnp.where(chosen > 0.5, dot(chosen.astype(BF16), before, 1, 0), -float(4 * tokens))

    def picked(expert_at, count, start):
        number = lax.broadcasted_iota(jnp.int32, (count, tokens), 0) - start
        return jnp.where(slots[pl.ds(expert_at, 1), :] == number.astype(F32), 1.0, 0.0)

    def gathered(expert_at, t, cols):
        chosen_rows = picked(expert_at, capacity, 0)
        gate = jnp.sum(chosen_rows * gate_rows[pl.ds(expert_at, 1), :], axis=1, keepdims=True)
        scale = jnp.where(t == 0, 1.0, gate)
        return (dot(chosen_rows.astype(BF16), base[t, :, cols], 1, 0) * scale).astype(BF16)

    pl.semaphore_wait(barrier, ctx_count + experts - 2)
    for p in remote:
        def run():
            for q in range(pieces):
                outgoing[p - 1, :, piece(q)] = gathered(chip_at(-order[p]) * 2 + near_core, x, piece(q))
                direct_copy(p, q).start()

        if_carrier(p, run)
    for t in range(2):
        to_partner[t] = gathered(partner, t, slice(None))
        partner_copy(t).start()

    loads[2].wait()
    loads[3].wait()

    def first_pass(h, carry):
        cols = head_cols(h)
        scores = dot(keys[:, cols], normed[:, cols], 1, 1) * HEAD ** (-0.5)
        peak = jnp.max(scores, axis=0, keepdims=True)
        weight = jnp.exp(scores - peak)
        slopes = dot(values[:, cols], upstream[:, cols], 1, 1)
        stats[0, pl.ds(h, 1), :] = peak
        stats[1, pl.ds(h, 1), :] = jnp.sum(weight, axis=0, keepdims=True)
        stats[2, pl.ds(h, 1), :] = jnp.sum(weight * slopes, axis=0, keepdims=True)
        return carry

    lax.fori_loop(0, HEADS, first_pass, 0, unroll=4)
    for d in range(1, ctx_count):
        stats_copy(d).start()
    for t in range(2):
        got[t, 0, k] = gathered(e, t, slice(None))

    chunk = 32

    def split(i, carry):
        at = pl.ds(pl.multiple_of(i * chunk, chunk), chunk)
        both = jnp.swapaxes(weights[at], 0, 1)
        w_in[at, :] = both[0]
        w_out[at, :] = both[1]
        return carry

    def second_pass(h, carry):
        cols = head_cols(h)
        key, q, g = keys[:, cols], normed[:, cols], upstream[:, cols]
        scores = dot(key, q, 1, 1) * HEAD ** (-0.5)
        probs = jnp.exp(scores - merged[0, pl.ds(h, 1), :]) / merged[1, pl.ds(h, 1), :]
        slopes = dot(values[:, cols], g, 1, 1)
        score_grad = (probs * (slopes - merged[2, pl.ds(h, 1), :])).astype(BF16)
        values_grad[:, cols] = dot(probs.astype(BF16), g, 1, 0).astype(BF16)
        keys_grad[:, cols] = (dot(score_grad, q, 1, 0) * HEAD ** (-0.5)).astype(BF16)
        query[:, cols] = dot(score_grad, key, 0, 0) * HEAD ** (-0.5)
        return carry

    steps = 4
    quarter = HEADS // steps

    def attend(i):
        lax.fori_loop(i * quarter, (i + 1) * quarter, second_pass, 0, unroll=quarter)

    def merge_stats():
        for d in range(1, ctx_count):
            stats_arrived(d).wait_recv()
        peak = stats[0]
        for d in range(ctx_count - 1):
            peak = jnp.maximum(peak, stats_all[d, 0])
        factor = jnp.exp(stats[0] - peak)
        denominator, inner = stats[1] * factor, stats[2] * factor
        for d in range(ctx_count - 1):
            factor = jnp.exp(stats_all[d, 0] - peak)
            denominator = denominator + stats_all[d, 1] * factor
            inner = inner + stats_all[d, 2] * factor
        merged[0] = peak
        merged[1] = denominator
        merged[2] = inner / denominator

    def forward(p, q):
        def run():
            direct_arrived(p, q).wait_recv()
            if q % 2 == 0:
                full_x_copy(p, q).start()
            for d in range(1, row_count):
                full_y_copy(p, d, q).start()
            if q % 2:
                full_x_copy(p, q).start()

        if_carrier(p, run)

    def forward_again(p, q):
        def run():
            full_arrived(p, 0, q).wait_recv()
            for d in range(1, row_count):
                second_y_copy(p, d, q).start()

        def other():
            full_arrived(p, 2, q).wait_recv()
            second_x_copy(p, 1, q).start()

        if q % 2 == 0:
            if_carrier(p, run)
        else:
            if_carrier(p, lambda: None, other)
            full_arrived(p, 1, q).wait_recv()
            second_x_copy(p, 0, q).start()

    def all_arrived(p):
        for q in range(pieces):
            def run():
                if q % 2:
                    full_arrived(p, 0, q).wait_recv()

            def other():
                if q % 2 == 0:
                    full_arrived(p, 2, q).wait_recv()
                second_arrived(p, 1, q).wait_recv()

            if_carrier(p, run, other)
            if q % 2 == 0:
                full_arrived(p, 1, q).wait_recv()
            second_arrived(p, 0, q).wait_recv()

    def pack(p):
        at = pl.ds(p * pair, pair)
        for t in range(2):
            rows[t, at, :] = got[t, p].reshape(pair, model_width)

    block = min(hidden, 256)
    step = HEAD * math.gcd(tiles, 5)

    def expert(group):
        at = pl.ds(group[0] * pair, len(group) * pair)
        for i in range(hidden // block):
            part = pl.ds(i * block, block)
            pre = dot(rows[0, at, :], w_in[part, :], 1, 1)
            act_grad = dot(rows[1, at, :], w_out[part, :], 1, 1)
            act, slope = gelu_pair(pre)
            activ[at, part] = act.astype(BF16)
            pre_grad[at, part] = (act_grad * slope).astype(BF16)
        for i in range(model_width // step):
            part = pl.ds(i * step, step)
            partial[at, part] = dot(pre_grad[at, :], w_in[:, part], 1, 0).astype(BF16)

    def share(owner):
        return pl.ds(pl.multiple_of(owner * tiles // ctx_count * HEAD, HEAD), width)

    def near_copy():
        return remote_copy(partial.at[pl.ds(0, pair), :], from_partner, near_sem, (0,), c, partner)

    def part_copy(p, d):
        peer = lax.rem(c + d, ctx_count)
        return remote_copy(
            partial.at[pl.ds(p * pair, pair), share(peer)], parts.at[p - 1, ctx_count - 1 - d],
            part_sem, (p, d - 1), peer, e,
        )

    def part_arrived(p, d):
        landed = parts.at[p - 1, ctx_count - 1 - d]
        return remote_copy(landed, landed, part_sem, (p, d - 1), c, partner)

    def back_position(p):
        return order.index((chips - order[p]) % chips)

    def back_copy(p, core):
        to = chip_at(order[p]) * 2 + core
        at = back_position(p)
        return pltpu.make_async_remote_copy(
            src_ref=reduced.at[p - 1, core], dst_ref=returned.at[at - 1, k],
            send_sem=back_sem.at[0, p, core], recv_sem=back_sem.at[1, at, k],
            device_id={"ctx": c, "exp": to}, device_id_type=MESH,
        )

    def back_arrived(p, core):
        landed = returned.at[p - 1, core]
        return remote_copy(landed, landed, back_sem, (p, core), c, partner)

    def local_copy(d):
        peer = lax.rem(c + d, ctx_count)
        return remote_copy(
            local_total.at[:, share(peer)], local_parts.at[ctx_count - 1 - d], local_sem, (d - 1,), peer, e
        )

    def local_arrived(d):
        landed = local_parts.at[ctx_count - 1 - d]
        return remote_copy(landed, landed, local_sem, (d - 1,), c, partner)

    def final_copy(d):
        peer = lax.rem(c + d, ctx_count)
        return remote_copy(finals.at[c], finals.at[c], final_sem, (d - 1,), peer, e)

    def final_arrived(d):
        landed = finals.at[lax.rem(c + ctx_count - d, ctx_count)]
        return remote_copy(landed, landed, final_sem, (d - 1,), c, partner)

    far_first = sorted(range(1, ctx_count), key=lambda d: d != ctx_count // 2)

    def send_parts(p):
        for d in far_first:
            part_copy(p, d).start()

    def reduce_parts(p):
        summed = partial[pl.ds(p * pair, pair), share(c)].astype(F32)
        for d in far_first:
            part_arrived(p, d).wait_recv()
        for d in range(ctx_count - 1):
            summed = summed + parts[p - 1, d].astype(F32)
        reduced[p - 1] = summed.astype(BF16).reshape(2, capacity, width)
        for core in range(2):
            back_copy(p, core).start()

    def near_total():
        near_copy().wait_recv()
        for i in range(model_width // step):
            part = pl.ds(i * step, step)
            local_total[:, part] = (
                query[:, part]
                + dot(select_near[0], partial[pl.ds(0, pair), part], 0, 0)
                + dot(select_near[1], from_partner[:, part], 0, 0)
            ).astype(BF16)

    def split_weights():
        loads[4].wait()
        lax.fori_loop(0, hidden // chunk, split, 0)

    def first_attend():
        merge_stats()
        attend(0)

    def last_attend():
        attend(steps - 1)
        for i in range(2):
            select_near[i] = picked((e, partner)[i], pair, k * capacity).astype(BF16)
        for p in remote:
            for core in range(2):
                select[p - 1, core] = picked(chip_at(order[p]) * 2 + core, capacity, 0).astype(BF16)
        for t in range(2):
            partner_arrived(t).wait_recv()
        pack(0)

    def run_group(group):
        for p in group:
            if p:
                all_arrived(p)
                pack(p)
        expert(group)
        for p in group:
            if p:
                send_parts(p)
            else:
                near_copy().start()
        if group[0] == 0:
            near_total()
        if group is groups[-1]:
            for d in far_first:
                local_copy(d).start()
        for p in pending:
            reduce_parts(p)
        pending[:] = [p for p in group if p]

    work = [split_weights, first_attend] + [functools.partial(attend, i) for i in range(1, steps - 1)] + [last_attend]
    pending = []
    moves = [(p, q) for p in remote for q in range(pieces)]
    lag, late = 1, 3
    for n in range(max(len(moves) + late, len(work))):
        if n < len(moves):
            forward(*moves[n])
        if n < len(work):
            work[n]()
        if 0 <= n - lag < len(moves):
            forward_again(*moves[n - lag])
        if 0 <= n - late < len(moves) and n >= len(work) - 1:
            for group in groups:
                if (group[-1], pieces - 1) == moves[n - late]:
                    run_group(group)
    for p in pending:
        reduce_parts(p)
    for d in far_first:
        local_arrived(d).wait_recv()
    summed = local_total[:, share(c)].astype(F32)
    for d in range(ctx_count - 1):
        summed = summed + local_parts[d].astype(F32)
    for p in sorted(remote, key=back_position):
        for core in range(2):
            back_arrived(p, core).wait_recv()
            summed = summed + dot(select[p - 1, core], returned[p - 1, core], 0, 0)
    finals[c] = summed.astype(BF16)
    for d in far_first:
        final_copy(d).start()
    for d in far_first:
        final_arrived(d).wait_recv()
    for owner in range(ctx_count):
        total[:, pl.ds(owner * tiles // ctx_count * HEAD, width)] = finals[owner]
    lines = 32

    def norm_gradient(i, carry):
        at = pl.ds(pl.multiple_of(i * lines, lines), lines)
        values_in = states[at, :].astype(F32)
        scale = lax.rsqrt(jnp.mean(values_in * values_in, axis=-1, keepdims=True) + EPSILON)
        unit = values_in * scale
        scaled = total[at, :].astype(F32) * gain[...][None]
        states_grad[at, :] = (
            upstream[at, :].astype(F32) + scale * (scaled - unit * jnp.mean(scaled * unit, axis=-1, keepdims=True))
        ).astype(BF16)
        return carry

    lax.fori_loop(0, tokens // lines, norm_gradient, 0)

    for t in range(2):
        partner_copy(t).wait_send()
    near_copy().wait_send()
    for d in range(1, ctx_count):
        stats_copy(d).wait_send()
        local_copy(d).wait_send()
        final_copy(d).wait_send()
    for p in remote:
        def run():
            for q in range(pieces):
                direct_copy(p, q).wait_send()
                full_x_copy(p, q).wait_send()
                for d in range(1, row_count):
                    full_y_copy(p, d, q).wait_send()
                    if q % 2 == 0:
                        second_y_copy(p, d, q).wait_send()

        def other():
            for q in range(1, pieces, 2):
                second_x_copy(p, 1, q).wait_send()

        if_carrier(p, run, other)
        for q in range(1, pieces, 2):
            second_x_copy(p, 0, q).wait_send()
        for core in range(2):
            back_copy(p, core).wait_send()
        for d in range(1, ctx_count):
            part_copy(p, d).wait_send()


def weights_kernel(
    pre_grad, activ, rows, states_grad, keys_grad, values_grad,
    weights_out, states_out, keys_out, values_out, grad, grad_sem, pass_sem,
):
    passed = [
        pltpu.make_async_copy(source, target, pass_sem.at[n])
        for n, (source, target) in enumerate(
            ((states_grad, states_out), (keys_grad, keys_out), (values_grad, values_out))
        )
    ]
    for copy in passed:
        copy.start()
    hidden = grad.shape[0]
    block = min(hidden, 128)

    def store(i):
        at = pl.ds(i * block, block)
        return pltpu.make_async_copy(grad.at[at], weights_out.at[at], grad_sem.at[i])

    for i in range(hidden // block):
        at = pl.ds(i * block, block)
        grad[at, 0, :] = dot(pre_grad[:, at], rows[0], 0, 0).astype(BF16)
        grad[at, 1, :] = dot(activ[:, at], rows[1], 0, 0).astype(BF16)
        store(i).start()
    for i in range(hidden // block):
        store(i).wait()
    for copy in passed:
        copy.wait()


def on_device(
    states, out_grad, doc_keys, doc_values, norm_gain, expert_ids, gate_values, expert_weights
):
    tokens, model_width = states.shape[1:]
    key_count = doc_keys.shape[1]
    ctx_count, experts = lax.axis_size("ctx"), lax.axis_size("exp")
    chips = experts // 2
    hidden = expert_weights.shape[1]
    capacity = 8 * -(-5 * TOP * tokens // (32 * experts))
    pair = 2 * capacity
    slot_rows = experts * capacity
    tiles = model_width // HEAD
    width = HEAD * max(-(-(c + 1) * tiles // ctx_count) - c * tiles // ctx_count for c in range(ctx_count))
    order = [0] + sorted(range(1, chips), key=lambda j: min(j, chips - j))
    pieces = 2
    groups = [[0, 1]] + [[p] for p in range(2, chips)]
    vmem = pl.BlockSpec(memory_space=pltpu.VMEM)
    hbm = pl.BlockSpec(memory_space=pltpu.HBM)
    shape = jax.ShapeDtypeStruct
    dma = pltpu.SemaphoreType.DMA
    near = max(chips - 1, 1)
    scratch = [
        ((tokens, model_width), BF16),
        ((tokens, model_width), BF16),
        ((key_count, model_width), BF16),
        ((key_count, model_width), BF16),
        ((hidden, 2, model_width), BF16),
        ((hidden, model_width), BF16),
        ((hidden, model_width), BF16),
        ((2, tokens, model_width), BF16),
        ((experts, tokens), F32),
        ((experts, tokens), F32),
        ((near, capacity, model_width), BF16),
        ((2, capacity, model_width), BF16),
        ((2, chips, 2, capacity, model_width), BF16),
        ((slot_rows, model_width), BF16),
        ((pair, model_width), BF16),
        ((near, 2, capacity, tokens), BF16),
        ((2, pair, tokens), BF16),
        ((tokens, model_width), F32),
        ((tokens, model_width), BF16),
        ((3, HEADS, tokens), F32),
        ((ctx_count - 1, 3, HEADS, tokens), F32),
        ((3, HEADS, tokens), F32),
        ((near, ctx_count - 1, pair, width), BF16),
        ((near, 2, capacity, width), BF16),
        ((near, 2, capacity, width), BF16),
        ((ctx_count - 1, tokens, width), BF16),
        ((ctx_count, tokens, width), BF16),
        ((tokens, model_width), BF16),
    ]
    semaphores = [
        (5,),
        (2, chips, pieces),
        (2, 2),
        (2, chips, max(ctx_count // 2, 3), pieces),
        (2, chips, ctx_count // 2 + 1, pieces),
        (2, ctx_count - 1),
        (2, 1),
        (2, chips, ctx_count - 1),
        (2, chips, 2),
        (2, ctx_count - 1),
        (2, ctx_count - 1),
    ]
    rows, pre_grad, activ, keys_grad, values_grad, states_grad = pl.pallas_call(
        functools.partial(block_kernel, ctx_count, experts, order, groups, pieces),
        out_shape=(
            shape((2, slot_rows, model_width), BF16),
            shape((slot_rows, hidden), BF16),
            shape((slot_rows, hidden), BF16),
            shape((key_count, model_width), BF16),
            shape((key_count, model_width), BF16),
            shape((tokens, model_width), BF16),
        ),
        in_specs=[vmem] * 3 + [hbm] * 5,
        out_specs=(vmem,) * 6,
        scratch_shapes=[pltpu.VMEM(s, t) for s, t in scratch] + [dma(s) for s in semaphores],
        compiler_params=pltpu.CompilerParams(
            vmem_limit_bytes=VMEM_LIMIT, collective_id=0, has_side_effects=True
        ),
    )(
        *(pltpu.with_memory_space_constraint(a, pltpu.HBM) for a in (norm_gain, expert_ids[0].T, gate_values[0].T)),
        *(pltpu.with_memory_space_constraint(a, pltpu.HBM) for a in (states[0], out_grad[0], doc_keys[0], doc_values[0], expert_weights[0])),
    )
    weights_grad, states_grad, keys_grad, values_grad = pl.pallas_call(
        weights_kernel,
        out_shape=(
            shape((hidden, 2, model_width), BF16),
            shape((tokens, model_width), BF16),
            shape((key_count, model_width), BF16),
            shape((key_count, model_width), BF16),
        ),
        in_specs=[vmem] * 6,
        out_specs=(hbm,) * 4,
        scratch_shapes=[
            pltpu.VMEM((hidden, 2, model_width), BF16),
            dma((-(-hidden // 128),)),
            dma((3,)),
        ],
        compiler_params=pltpu.CompilerParams(vmem_limit_bytes=SECOND_LIMIT),
    )(pre_grad, activ, rows, states_grad, keys_grad, values_grad)
    return states_grad[None], keys_grad[None], values_grad[None], weights_grad[None]


def solution(mesh):
    return jax.shard_map(
        on_device,
        mesh=mesh,
        in_specs=(
            P("exp", None, None),
            P("exp", None, None),
            P("exp", "ctx", None),
            P("exp", "ctx", None),
            P(),
            P("exp", None, None),
            P("exp", None, None),
            P("exp", "ctx", None, None),
        ),
        out_specs=(
            P("exp", None, None),
            P("exp", "ctx", None),
            P("exp", "ctx", None),
            P("exp", "ctx", None, None),
        ),
        check_vma=False,
    )
```

```python
import functools
import math
import jax
import jax.numpy as jnp
from jax import lax
from jax.experimental import pallas as pl
from jax.experimental.pallas import tpu as pltpu
from jax.sharding import PartitionSpec as P

HEADS = 20
HEAD = 128
TOP = 2


EPSILON = 1e-05
MESH = pl.DeviceIdType.MESH
F32 = jnp.float32
BF16 = jnp.bfloat16
VMEM_LIMIT = 44 * 1024 * 1024
SECOND_LIMIT = 24 * 1024 * 1024


def dot(a, b, ca, cb):
    return lax.dot_general(a, b, (((ca,), (cb,)), ((), ())), preferred_element_type=F32)


def head_cols(h):
    return pl.ds(pl.multiple_of(h * HEAD, HEAD), HEAD)


def gelu_pair(v):
    slope, cubic = math.sqrt(2.0 / math.pi), 0.044715
    square = v * v
    tanh = jnp.tanh(slope * v * (1.0 + cubic * square))
    half = 0.5 * (1.0 + tanh)
    inner = slope * (1.0 + 3.0 * cubic * square)
    return v * half, half + 0.5 * v * (1.0 - tanh * tanh) * inner


def block_kernel(
    ctx_count, experts, order, groups, pieces, whole,
    gain, ids, gates, states_hbm, upstream_hbm, keys_hbm, values_hbm, weights_hbm,
    rows, pre_grad, activ, keys_grad, values_grad, states_grad,
    states, upstream, keys, values, weights, w_in, w_out, base, slots, gate_rows, outgoing, to_partner,
    got, partial, whole_rows, whole_got, from_partner, select, select_near, query, local_total,
    stats, stats_all, merged,
    parts, reduced, returned, local_parts, finals, total,
    load_sem, direct_sem, partner_sem, full_sem, second_sem, stats_sem,
    near_sem, whole_sem, part_sem, back_sem, local_sem, final_sem,
):
    c, e = lax.axis_index("ctx"), lax.axis_index("exp")
    chips = experts // 2
    tokens, model_width = states.shape
    capacity = got.shape[3]
    hidden = w_in.shape[0]
    pair = 2 * capacity
    width = finals.shape[2]
    tiles = model_width // HEAD
    row_count = ctx_count // 2
    sets = row_count // 2
    x, y = lax.rem(c, 2), c // 2
    z, k = e // 2, lax.rem(e, 2)
    remote = range(1, chips)
    x_peer, partner = y * 2 + (1 - x), z * 2 + (1 - k)
    near_core, far_core = lax.rem(k + y, 2), lax.rem(k + 1 + y, 2)

    def chip_at(offset):
        return lax.rem(z + offset + chips, chips)

    def row_peer(d):
        return lax.rem(y + d, row_count) * 2 + x

    def if_carrier(p, run, other=None):
        if sets == 1:
            run()
        else:
            carrier = y // 2 == p % sets
            pl.when(carrier)(run)
            if other is not None:
                pl.when(jnp.logical_not(carrier))(other)

    def remote_copy(src, dst, sem, at, to_c, to_e, got_at=None):
        return pltpu.make_async_remote_copy(
            src_ref=src, dst_ref=dst,
            send_sem=sem.at[(0, *at)], recv_sem=sem.at[(1, *(at if got_at is None else got_at))],
            device_id={"ctx": to_c, "exp": to_e}, device_id_type=MESH,
        )

    loads = [
        pltpu.make_async_copy(source, target, load_sem.at[n])
        for n, (source, target) in enumerate((
            (states_hbm, states), (upstream_hbm, upstream), (keys_hbm, keys),
            (values_hbm, values), (weights_hbm, weights),
        ))
    ]
    for load in loads:
        load.start()

    barrier = pltpu.get_barrier_semaphore()
    for d in range(1, ctx_count):
        pl.semaphore_signal(barrier, inc=1, device_id={"ctx": lax.rem(c + d, ctx_count), "exp": e}, device_id_type=MESH)
    for d in range(1, experts):
        pl.semaphore_signal(barrier, inc=1, device_id={"ctx": c, "exp": lax.rem(e + d, experts)}, device_id_type=MESH)

    def piece(q):
        start, end = (at * tiles // pieces * HEAD for at in (q, q + 1))
        return pl.ds(start, end - start)

    def direct_copy(p, q):
        to = chip_at(-order[p]) * 2 + near_core
        return remote_copy(
            outgoing.at[p - 1, :, piece(q)], got.at[x, p, k].at[:, piece(q)], direct_sem, (p, q), c, to
        )

    def direct_arrived(p, q):
        landed = got.at[x, p, near_core].at[:, piece(q)]
        return remote_copy(landed, landed, direct_sem, (p, q), c, partner)

    def partner_copy(t):
        return remote_copy(to_partner.at[t], got.at[t, 0, k], partner_sem, (t,), c, partner)

    def partner_arrived(t):
        landed = got.at[t, 0, 1 - k]
        return remote_copy(landed, landed, partner_sem, (t,), c, partner)

    def full_x_copy(p, q):
        block = got.at[x, p, near_core].at[:, piece(q)]
        return remote_copy(block, block, full_sem, (p, 0, q), x_peer, e)

    def full_y_copy(p, d, q):
        block = got.at[x, p, near_core].at[:, piece(q)]
        return remote_copy(block, block, full_sem, (p, d, q), row_peer(d), e, (p, 2 - d % 2, q))

    def full_block(p, way, q):
        block = (got.at[1 - x, p, near_core], got.at[x, p, far_core], got.at[x, p, near_core])[way]
        return block.at[:, piece(q)]

    def full_arrived(p, way, q):
        landed = full_block(p, way, q)
        return remote_copy(landed, landed, full_sem, (p, way, q), c, partner)

    def second_y_copy(p, d, q):
        block = got.at[1 - x, p, near_core].at[:, piece(q)]
        return remote_copy(block, block, second_sem, (p, d + 1, q), row_peer(d), e, (p, 1 - d % 2, q))

    def second_x_copy(p, even, q):
        block = full_block(p, 1 + even, q)
        return remote_copy(block, block, second_sem, (p, even, q), x_peer, e)

    def second_arrived(p, even, q):
        landed = got.at[1 - x, p, (far_core, near_core)[even]].at[:, piece(q)]
        return remote_copy(landed, landed, second_sem, (p, even, q), c, partner)

    def stats_copy(d):
        return remote_copy(
            stats, stats_all.at[ctx_count - 1 - d], stats_sem, (d - 1,), lax.rem(c + d, ctx_count), e
        )

    def stats_arrived(d):
        landed = stats_all.at[ctx_count - 1 - d]
        return remote_copy(landed, landed, stats_sem, (d - 1,), c, partner)

    loads[0].wait()
    loads[1].wait()
    inputs = states[...].astype(F32)
    inverse = lax.rsqrt(jnp.mean(inputs * inputs, axis=-1, keepdims=True) + EPSILON)
    base[0] = (inputs * inverse * gain[...][None]).astype(BF16)
    base[1] = upstream[...]
    normed = base.at[0]
    expert = lax.broadcasted_iota(jnp.int32, (experts, tokens), 0)
    first, second = ids[0:1, :] == expert, ids[1:2, :] == expert
    chosen = jnp.where(first | second, 1.0, 0.0)
    gate_rows[...] = jnp.where(first, gates[0:1, :], jnp.where(second, gates[1:2, :], 0.0))
    before = jnp.where(
        lax.broadcasted_iota(jnp.int32, (tokens, tokens), 0) < lax.broadcasted_iota(jnp.int32, (tokens, tokens), 1),
        1.0, 0.0,
    ).astype(BF16)
    slots[...] = jnp.where(chosen > 0.5, dot(chosen.astype(BF16), before, 1, 0), -float(4 * tokens))

    def picked(expert_at, count, start):
        number = lax.broadcasted_iota(jnp.int32, (count, tokens), 0) - start
        return jnp.where(slots[pl.ds(expert_at, 1), :] == number.astype(F32), 1.0, 0.0)

    def gathered(expert_at, t, cols):
        chosen_rows = picked(expert_at, capacity, 0)
        gate = jnp.sum(chosen_rows * gate_rows[pl.ds(expert_at, 1), :], axis=1, keepdims=True)
        scale = jnp.where(t == 0, 1.0, gate)
        return (dot(chosen_rows.astype(BF16), base[t, :, cols], 1, 0) * scale).astype(BF16)

    pl.semaphore_wait(barrier, ctx_count + experts - 2)
    for p in remote:
        def run():
            for q in range(pieces):
                outgoing[p - 1, :, piece(q)] = gathered(chip_at(-order[p]) * 2 + near_core, x, piece(q))
                direct_copy(p, q).start()

        if_carrier(p, run)
    for t in range(2):
        to_partner[t] = gathered(partner, t, slice(None))
        partner_copy(t).start()

    loads[2].wait()
    loads[3].wait()

    def first_pass(h, carry):
        cols = head_cols(h)
        scores = dot(keys[:, cols], normed[:, cols], 1, 1) * HEAD ** (-0.5)
        peak = jnp.max(scores, axis=0, keepdims=True)
        weight = jnp.exp(scores - peak)
        slopes = dot(values[:, cols], upstream[:, cols], 1, 1)
        stats[0, pl.ds(h, 1), :] = peak
        stats[1, pl.ds(h, 1), :] = jnp.sum(weight, axis=0, keepdims=True)
        stats[2, pl.ds(h, 1), :] = jnp.sum(weight * slopes, axis=0, keepdims=True)
        return carry

    lax.fori_loop(0, HEADS, first_pass, 0, unroll=4)
    for d in range(1, ctx_count):
        stats_copy(d).start()
    for t in range(2):
        got[t, 0, k] = gathered(e, t, slice(None))

    chunk = 32

    def split(i, carry):
        at = pl.ds(pl.multiple_of(i * chunk, chunk), chunk)
        both = jnp.swapaxes(weights[at], 0, 1)
        w_in[at, :] = both[0]
        w_out[at, :] = both[1]
        return carry

    def second_pass(h, carry):
        cols = head_cols(h)
        key, q, g = keys[:, cols], normed[:, cols], upstream[:, cols]
        scores = dot(key, q, 1, 1) * HEAD ** (-0.5)
        probs = jnp.exp(scores - merged[0, pl.ds(h, 1), :]) / merged[1, pl.ds(h, 1), :]
        slopes = dot(values[:, cols], g, 1, 1)
        score_grad = (probs * (slopes - merged[2, pl.ds(h, 1), :])).astype(BF16)
        values_grad[:, cols] = dot(probs.astype(BF16), g, 1, 0).astype(BF16)
        keys_grad[:, cols] = (dot(score_grad, q, 1, 0) * HEAD ** (-0.5)).astype(BF16)
        query[:, cols] = dot(score_grad, key, 0, 0) * HEAD ** (-0.5)
        return carry

    steps = 4
    quarter = HEADS // steps

    def attend(i):
        lax.fori_loop(i * quarter, (i + 1) * quarter, second_pass, 0, unroll=quarter)

    def merge_stats():
        for d in range(1, ctx_count):
            stats_arrived(d).wait_recv()
        peak = stats[0]
        for d in range(ctx_count - 1):
            peak = jnp.maximum(peak, stats_all[d, 0])
        factor = jnp.exp(stats[0] - peak)
        denominator, inner = stats[1] * factor, stats[2] * factor
        for d in range(ctx_count - 1):
            factor = jnp.exp(stats_all[d, 0] - peak)
            denominator = denominator + stats_all[d, 1] * factor
            inner = inner + stats_all[d, 2] * factor
        merged[0] = peak
        merged[1] = denominator
        merged[2] = inner / denominator

    def forward(p, q):
        def run():
            direct_arrived(p, q).wait_recv()
            if q % 2 == 0:
                full_x_copy(p, q).start()
            for d in range(1, row_count):
                full_y_copy(p, d, q).start()
            if q % 2:
                full_x_copy(p, q).start()

        if_carrier(p, run)

    def forward_again(p, q):
        def run():
            full_arrived(p, 0, q).wait_recv()
            for d in range(1, row_count):
                second_y_copy(p, d, q).start()

        def other():
            full_arrived(p, 2, q).wait_recv()
            second_x_copy(p, 1, q).start()

        if q % 2 == 0:
            if_carrier(p, run)
        else:
            if_carrier(p, lambda: None, other)
            full_arrived(p, 1, q).wait_recv()
            second_x_copy(p, 0, q).start()

    def all_arrived(p):
        for q in range(pieces):
            def run():
                if q % 2:
                    full_arrived(p, 0, q).wait_recv()

            def other():
                if q % 2 == 0:
                    full_arrived(p, 2, q).wait_recv()
                second_arrived(p, 1, q).wait_recv()

            if_carrier(p, run, other)
            if q % 2 == 0:
                full_arrived(p, 1, q).wait_recv()
            second_arrived(p, 0, q).wait_recv()

    def pack(p):
        at = pl.ds(p * pair, pair)
        for t in range(2):
            rows[t, at, :] = got[t, p].reshape(pair, model_width)

    block = min(hidden, 256)
    step = HEAD * math.gcd(tiles, 5)

    def expert(group):
        at = pl.ds(group[0] * pair, len(group) * pair)
        for i in range(hidden // block):
            part = pl.ds(i * block, block)
            pre = dot(rows[0, at, :], w_in[part, :], 1, 1)
            act_grad = dot(rows[1, at, :], w_out[part, :], 1, 1)
            act, slope = gelu_pair(pre)
            activ[at, part] = act.astype(BF16)
            pre_grad[at, part] = (act_grad * slope).astype(BF16)
        for i in range(model_width // step):
            part = pl.ds(i * step, step)
            piece_rows = dot(pre_grad[at, :], w_in[:, part], 1, 0).astype(BF16)
            for n, p in enumerate(group):
                own = piece_rows[n * pair : (n + 1) * pair]
                if p == whole:
                    whole_rows[:, :, part] = own.reshape(2, capacity, step)
                else:
                    partial[pl.ds(p * pair, pair), part] = own

    def share(owner):
        return pl.ds(pl.multiple_of(owner * tiles // ctx_count * HEAD, HEAD), width)

    def near_copy():
        return remote_copy(partial.at[pl.ds(0, pair), :], from_partner, near_sem, (0,), c, partner)

    def part_copy(p, d):
        peer = lax.rem(c + d, ctx_count)
        return remote_copy(
            partial.at[pl.ds(p * pair, pair), share(peer)], parts.at[p - 1, ctx_count - 1 - d],
            part_sem, (p, d - 1), peer, e,
        )

    def part_arrived(p, d):
        landed = parts.at[p - 1, ctx_count - 1 - d]
        return remote_copy(landed, landed, part_sem, (p, d - 1), c, partner)

    def back_position(p):
        return order.index((chips - order[p]) % chips)

    def back_copy(p, core):
        to = chip_at(order[p]) * 2 + core
        at = back_position(p)
        return pltpu.make_async_remote_copy(
            src_ref=reduced.at[p - 1, core], dst_ref=returned.at[at - 1, k],
            send_sem=back_sem.at[0, p, core], recv_sem=back_sem.at[1, at, k],
            device_id={"ctx": c, "exp": to}, device_id_type=MESH,
        )

    def back_arrived(p, core):
        landed = returned.at[p - 1, core]
        return remote_copy(landed, landed, back_sem, (p, core), c, partner)

    def whole_copy(core):
        to = chip_at(order[whole]) * 2 + core
        return pltpu.make_async_remote_copy(
            src_ref=whole_rows.at[core], dst_ref=whole_got.at[k],
            send_sem=whole_sem.at[0, core], recv_sem=whole_sem.at[1, k],
            device_id={"ctx": c, "exp": to}, device_id_type=MESH,
        )

    def whole_arrived(core):
        landed = whole_got.at[core]
        return remote_copy(landed, landed, whole_sem, (core,), c, partner)

    def local_copy(d):
        peer = lax.rem(c + d, ctx_count)
        return remote_copy(
            local_total.at[:, share(peer)], local_parts.at[ctx_count - 1 - d], local_sem, (d - 1,), peer, e
        )

    def local_arrived(d):
        landed = local_parts.at[ctx_count - 1 - d]
        return remote_copy(landed, landed, local_sem, (d - 1,), c, partner)

    def final_copy(d):
        peer = lax.rem(c + d, ctx_count)
        return remote_copy(finals.at[c], finals.at[c], final_sem, (d - 1,), peer, e)

    def final_arrived(d):
        landed = finals.at[lax.rem(c + ctx_count - d, ctx_count)]
        return remote_copy(landed, landed, final_sem, (d - 1,), c, partner)

    far_first = sorted(range(1, ctx_count), key=lambda d: d != ctx_count // 2)

    def send_parts(p):
        for d in far_first:
            part_copy(p, d).start()

    def reduce_parts(p):
        summed = partial[pl.ds(p * pair, pair), share(c)].astype(F32)
        for d in far_first:
            part_arrived(p, d).wait_recv()
        for d in range(ctx_count - 1):
            summed = summed + parts[p - 1, d].astype(F32)
        reduced[p - 1] = summed.astype(BF16).reshape(2, capacity, width)
        for core in range(2):
            back_copy(p, core).start()

    def near_total():
        near_copy().wait_recv()
        for i in range(model_width // step):
            part = pl.ds(i * step, step)
            query[:, part] += dot(select_near[0], partial[pl.ds(0, pair), part], 0, 0) + dot(
                select_near[1], from_partner[:, part], 0, 0
            )

    def send_total():
        for core in range(2):
            whole_arrived(core).wait_recv()
        for i in range(model_width // step):
            part = pl.ds(i * step, step)
            summed = query[:, part]
            for core in range(2):
                summed += dot(select[back_position(whole) - 1, core], whole_got[core, :, part], 0, 0)
            local_total[:, part] = summed.astype(BF16)
        for d in far_first:
            local_copy(d).start()

    def split_weights():
        loads[4].wait()
        lax.fori_loop(0, hidden // chunk, split, 0)

    def first_attend():
        merge_stats()
        attend(0)

    def last_attend():
        attend(steps - 1)
        for i in range(2):
            select_near[i] = picked((e, partner)[i], pair, k * capacity).astype(BF16)
        for p in remote:
            for core in range(2):
                select[p - 1, core] = picked(chip_at(order[p]) * 2 + core, capacity, 0).astype(BF16)
        for t in range(2):
            partner_arrived(t).wait_recv()
        pack(0)

    def run_group(group):
        for p in group:
            if p:
                all_arrived(p)
                pack(p)
        expert(group)
        for p in group:
            if p == whole:
                for core in range(2):
                    whole_copy(core).start()
            elif p:
                send_parts(p)
            else:
                near_copy().start()
        if group[0] == 0:
            near_total()
        if group is groups[-1]:
            send_total()
        for p in pending:
            reduce_parts(p)
        pending[:] = [p for p in group if p and p != whole]

    work = [split_weights, first_attend] + [functools.partial(attend, i) for i in range(1, steps - 1)] + [last_attend]
    pending, waiting = [], list(groups)
    moves = [(p, q) for p in remote for q in range(pieces)]
    stride, lag, late = 1, 2, 4
    for n in range(max(len(moves) + late, len(work) * stride)):
        if n < len(moves):
            forward(*moves[n])
        if n % stride == 0 and n // stride < len(work):
            work[n // stride]()
        if 0 <= n - lag < len(moves):
            forward_again(*moves[n - lag])
        while waiting and n >= (len(work) - 1) * stride and moves.index((waiting[0][-1], pieces - 1)) <= n - late:
            run_group(waiting.pop(0))
    for p in pending:
        reduce_parts(p)
    for d in far_first:
        local_arrived(d).wait_recv()
    summed = local_total[:, share(c)].astype(F32)
    for d in range(ctx_count - 1):
        summed = summed + local_parts[d].astype(F32)
    for p in sorted(set(remote) - {back_position(whole)}, key=back_position):
        for core in range(2):
            back_arrived(p, core).wait_recv()
            summed = summed + dot(select[p - 1, core], returned[p - 1, core], 0, 0)
    finals[c] = summed.astype(BF16)
    for d in far_first:
        final_copy(d).start()
    for d in far_first:
        final_arrived(d).wait_recv()
    for owner in range(ctx_count):
        total[:, pl.ds(owner * tiles // ctx_count * HEAD, width)] = finals[owner]
    lines = 32

    def norm_gradient(i, carry):
        at = pl.ds(pl.multiple_of(i * lines, lines), lines)
        values_in = states[at, :].astype(F32)
        scale = lax.rsqrt(jnp.mean(values_in * values_in, axis=-1, keepdims=True) + EPSILON)
        unit = values_in * scale
        scaled = total[at, :].astype(F32) * gain[...][None]
        states_grad[at, :] = (
            upstream[at, :].astype(F32) + scale * (scaled - unit * jnp.mean(scaled * unit, axis=-1, keepdims=True))
        ).astype(BF16)
        return carry

    lax.fori_loop(0, tokens // lines, norm_gradient, 0)

    for t in range(2):
        partner_copy(t).wait_send()
    near_copy().wait_send()
    for d in range(1, ctx_count):
        stats_copy(d).wait_send()
        local_copy(d).wait_send()
        final_copy(d).wait_send()
    for p in remote:
        def run():
            for q in range(pieces):
                direct_copy(p, q).wait_send()
                full_x_copy(p, q).wait_send()
                for d in range(1, row_count):
                    full_y_copy(p, d, q).wait_send()
                    if q % 2 == 0:
                        second_y_copy(p, d, q).wait_send()

        def other():
            for q in range(1, pieces, 2):
                second_x_copy(p, 1, q).wait_send()

        if_carrier(p, run, other)
        for q in range(1, pieces, 2):
            second_x_copy(p, 0, q).wait_send()
        for core in range(2):
            (whole_copy(core) if p == whole else back_copy(p, core)).wait_send()
        for d in range(1, ctx_count):
            if p != whole:
                part_copy(p, d).wait_send()


def weights_kernel(
    pre_grad, activ, rows, states_grad, keys_grad, values_grad,
    weights_out, states_out, keys_out, values_out, grad, grad_sem, pass_sem,
):
    passed = [
        pltpu.make_async_copy(source, target, pass_sem.at[n])
        for n, (source, target) in enumerate(
            ((states_grad, states_out), (keys_grad, keys_out), (values_grad, values_out))
        )
    ]
    for copy in passed:
        copy.start()
    hidden = grad.shape[0]
    block = min(hidden, 128)

    def store(i):
        at = pl.ds(i * block, block)
        return pltpu.make_async_copy(grad.at[at], weights_out.at[at], grad_sem.at[i])

    for i in range(hidden // block):
        at = pl.ds(i * block, block)
        grad[at, 0, :] = dot(pre_grad[:, at], rows[0], 0, 0).astype(BF16)
        grad[at, 1, :] = dot(activ[:, at], rows[1], 0, 0).astype(BF16)
        store(i).start()
    for i in range(hidden // block):
        store(i).wait()
    for copy in passed:
        copy.wait()


def on_device(
    states, out_grad, doc_keys, doc_values, norm_gain, expert_ids, gate_values, expert_weights
):
    tokens, model_width = states.shape[1:]
    key_count = doc_keys.shape[1]
    ctx_count, experts = lax.axis_size("ctx"), lax.axis_size("exp")
    chips = experts // 2
    hidden = expert_weights.shape[1]
    capacity = 8 * -(-5 * TOP * tokens // (32 * experts))
    pair = 2 * capacity
    slot_rows = experts * capacity
    tiles = model_width // HEAD
    width = HEAD * max(-(-(c + 1) * tiles // ctx_count) - c * tiles // ctx_count for c in range(ctx_count))
    order = [0] + sorted(range(1, chips), key=lambda j: min(j, chips - j))
    pieces = 2
    groups = [[0, 1]] + [[p] for p in range(2, chips)]
    vmem = pl.BlockSpec(memory_space=pltpu.VMEM)
    hbm = pl.BlockSpec(memory_space=pltpu.HBM)
    shape = jax.ShapeDtypeStruct
    dma = pltpu.SemaphoreType.DMA
    near = max(chips - 1, 1)
    scratch = [
        ((tokens, model_width), BF16),
        ((tokens, model_width), BF16),
        ((key_count, model_width), BF16),
        ((key_count, model_width), BF16),
        ((hidden, 2, model_width), BF16),
        ((hidden, model_width), BF16),
        ((hidden, model_width), BF16),
        ((2, tokens, model_width), BF16),
        ((experts, tokens), F32),
        ((experts, tokens), F32),
        ((near, capacity, model_width), BF16),
        ((2, capacity, model_width), BF16),
        ((2, chips, 2, capacity, model_width), BF16),
        ((slot_rows, model_width), BF16),
        ((2, capacity, model_width), BF16),
        ((2, capacity, model_width), BF16),
        ((pair, model_width), BF16),
        ((near, 2, capacity, tokens), BF16),
        ((2, pair, tokens), BF16),
        ((tokens, model_width), F32),
        ((tokens, model_width), BF16),
        ((3, HEADS, tokens), F32),
        ((ctx_count - 1, 3, HEADS, tokens), F32),
        ((3, HEADS, tokens), F32),
        ((near, ctx_count - 1, pair, width), BF16),
        ((near, 2, capacity, width), BF16),
        ((near, 2, capacity, width), BF16),
        ((ctx_count - 1, tokens, width), BF16),
        ((ctx_count, tokens, width), BF16),
        ((tokens, model_width), BF16),
    ]
    semaphores = [
        (5,),
        (2, chips, pieces),
        (2, 2),
        (2, chips, max(ctx_count // 2, 3), pieces),
        (2, chips, ctx_count // 2 + 1, pieces),
        (2, ctx_count - 1),
        (2, 1),
        (2, 2),
        (2, chips, ctx_count - 1),
        (2, chips, 2),
        (2, ctx_count - 1),
        (2, ctx_count - 1),
    ]
    rows, pre_grad, activ, keys_grad, values_grad, states_grad = pl.pallas_call(
        functools.partial(block_kernel, ctx_count, experts, order, groups, pieces, 1),
        out_shape=(
            shape((2, slot_rows, model_width), BF16),
            shape((slot_rows, hidden), BF16),
            shape((slot_rows, hidden), BF16),
            shape((key_count, model_width), BF16),
            shape((key_count, model_width), BF16),
            shape((tokens, model_width), BF16),
        ),
        in_specs=[vmem] * 3 + [hbm] * 5,
        out_specs=(vmem,) * 6,
        scratch_shapes=[pltpu.VMEM(s, t) for s, t in scratch] + [dma(s) for s in semaphores],
        compiler_params=pltpu.CompilerParams(
            vmem_limit_bytes=VMEM_LIMIT, collective_id=0, has_side_effects=True
        ),
    )(
        *(pltpu.with_memory_space_constraint(a, pltpu.HBM) for a in (norm_gain, expert_ids[0].T, gate_values[0].T)),
        *(pltpu.with_memory_space_constraint(a, pltpu.HBM) for a in (states[0], out_grad[0], doc_keys[0], doc_values[0], expert_weights[0])),
    )
    weights_grad, states_grad, keys_grad, values_grad = pl.pallas_call(
        weights_kernel,
        out_shape=(
            shape((hidden, 2, model_width), BF16),
            shape((tokens, model_width), BF16),
            shape((key_count, model_width), BF16),
            shape((key_count, model_width), BF16),
        ),
        in_specs=[vmem] * 6,
        out_specs=(hbm,) * 4,
        scratch_shapes=[
            pltpu.VMEM((hidden, 2, model_width), BF16),
            dma((-(-hidden // 128),)),
            dma((3,)),
        ],
        compiler_params=pltpu.CompilerParams(vmem_limit_bytes=SECOND_LIMIT),
    )(pre_grad, activ, rows, states_grad, keys_grad, values_grad)
    return states_grad[None], keys_grad[None], values_grad[None], weights_grad[None]


def solution(mesh):
    return jax.shard_map(
        on_device,
        mesh=mesh,
        in_specs=(
            P("exp", None, None),
            P("exp", None, None),
            P("exp", "ctx", None),
            P("exp", "ctx", None),
            P(),
            P("exp", None, None),
            P("exp", None, None),
            P("exp", "ctx", None, None),
        ),
        out_specs=(
            P("exp", None, None),
            P("exp", "ctx", None),
            P("exp", "ctx", None),
            P("exp", "ctx", None, None),
        ),
        check_vma=False,
    )
```

```python
import functools
import math
import jax
import jax.numpy as jnp
from jax import lax
from jax.experimental import pallas as pl
from jax.experimental.pallas import tpu as pltpu
from jax.sharding import PartitionSpec as P

HEADS = 20
HEAD = 128
TOP = 2


EPSILON = 1e-05
MESH = pl.DeviceIdType.MESH
F32 = jnp.float32
BF16 = jnp.bfloat16
VMEM_LIMIT = 44 * 1024 * 1024
SECOND_LIMIT = 24 * 1024 * 1024


def dot(a, b, ca, cb):
    return lax.dot_general(a, b, (((ca,), (cb,)), ((), ())), preferred_element_type=F32)


def head_cols(h):
    return pl.ds(pl.multiple_of(h * HEAD, HEAD), HEAD)


def gelu_pair(v):
    slope, cubic = math.sqrt(2.0 / math.pi), 0.044715
    square = v * v
    tanh = jnp.tanh(slope * v * (1.0 + cubic * square))
    half = 0.5 * (1.0 + tanh)
    inner = slope * (1.0 + 3.0 * cubic * square)
    return v * half, half + 0.5 * v * (1.0 - tanh * tanh) * inner


def block_kernel(
    ctx_count, experts, order, groups, pieces, whole,
    gain, ids, gates, states_hbm, upstream_hbm, keys_hbm, values_hbm, weights_hbm,
    rows, pre_grad, activ, keys_grad, values_grad, states_grad,
    states, upstream, keys, values, weights, w_in, w_out, base, slots, gate_rows, outgoing, to_partner,
    got, partial, whole_rows, whole_got, from_partner, select, select_near, query, local_total,
    stats, stats_all, merged,
    parts, reduced, returned, local_parts, finals, total,
    load_sem, direct_sem, partner_sem, full_sem, second_sem, stats_sem,
    near_sem, whole_sem, part_sem, back_sem, local_sem, final_sem,
):
    c, e = lax.axis_index("ctx"), lax.axis_index("exp")
    chips = experts // 2
    tokens, model_width = states.shape
    capacity = got.shape[3]
    hidden = w_in.shape[0]
    pair = 2 * capacity
    width = finals.shape[2]
    tiles = model_width // HEAD
    row_count = ctx_count // 2
    sets = row_count // 2
    x, y = lax.rem(c, 2), c // 2
    z, k = e // 2, lax.rem(e, 2)
    remote = range(1, chips)
    x_peer, partner = y * 2 + (1 - x), z * 2 + (1 - k)
    near_core, far_core = lax.rem(k + y, 2), lax.rem(k + 1 + y, 2)

    def chip_at(offset):
        return lax.rem(z + offset + chips, chips)

    def row_peer(d):
        return lax.rem(y + d, row_count) * 2 + x

    def if_carrier(p, run, other=None):
        if sets == 1:
            run()
        else:
            carrier = y // 2 == p % sets
            pl.when(carrier)(run)
            if other is not None:
                pl.when(jnp.logical_not(carrier))(other)

    def remote_copy(src, dst, sem, at, to_c, to_e, got_at=None):
        return pltpu.make_async_remote_copy(
            src_ref=src, dst_ref=dst,
            send_sem=sem.at[(0, *at)], recv_sem=sem.at[(1, *(at if got_at is None else got_at))],
            device_id={"ctx": to_c, "exp": to_e}, device_id_type=MESH,
        )

    loads = [
        pltpu.make_async_copy(source, target, load_sem.at[n])
        for n, (source, target) in enumerate((
            (states_hbm, states), (upstream_hbm, upstream), (keys_hbm, keys),
            (values_hbm, values), (weights_hbm, weights),
        ))
    ]
    for load in loads:
        load.start()

    barrier = pltpu.get_barrier_semaphore()
    for d in range(1, ctx_count):
        pl.semaphore_signal(barrier, inc=1, device_id={"ctx": lax.rem(c + d, ctx_count), "exp": e}, device_id_type=MESH)
    for d in range(1, experts):
        pl.semaphore_signal(barrier, inc=1, device_id={"ctx": c, "exp": lax.rem(e + d, experts)}, device_id_type=MESH)

    def piece(q):
        start, end = (at * tiles // pieces * HEAD for at in (q, q + 1))
        return pl.ds(start, end - start)

    def direct_copy(p, q):
        to = chip_at(-order[p]) * 2 + near_core
        return remote_copy(
            outgoing.at[p - 1, :, piece(q)], got.at[x, p, k].at[:, piece(q)], direct_sem, (p, q), c, to
        )

    def direct_arrived(p, q):
        landed = got.at[x, p, near_core].at[:, piece(q)]
        return remote_copy(landed, landed, direct_sem, (p, q), c, partner)

    def partner_copy(t):
        return remote_copy(to_partner.at[t], got.at[t, 0, k], partner_sem, (t,), c, partner)

    def partner_arrived(t):
        landed = got.at[t, 0, 1 - k]
        return remote_copy(landed, landed, partner_sem, (t,), c, partner)

    def full_x_copy(p, q):
        block = got.at[x, p, near_core].at[:, piece(q)]
        return remote_copy(block, block, full_sem, (p, 0, q), x_peer, e)

    def full_y_copy(p, d, q):
        block = got.at[x, p, near_core].at[:, piece(q)]
        return remote_copy(block, block, full_sem, (p, d, q), row_peer(d), e, (p, 2 - d % 2, q))

    def full_block(p, way, q):
        block = (got.at[1 - x, p, near_core], got.at[x, p, far_core], got.at[x, p, near_core])[way]
        return block.at[:, piece(q)]

    def full_arrived(p, way, q):
        landed = full_block(p, way, q)
        return remote_copy(landed, landed, full_sem, (p, way, q), c, partner)

    def second_y_copy(p, d, q):
        block = got.at[1 - x, p, near_core].at[:, piece(q)]
        return remote_copy(block, block, second_sem, (p, d + 1, q), row_peer(d), e, (p, 1 - d % 2, q))

    def second_x_copy(p, even, q):
        block = full_block(p, 1 + even, q)
        return remote_copy(block, block, second_sem, (p, even, q), x_peer, e)

    def second_arrived(p, even, q):
        landed = got.at[1 - x, p, (far_core, near_core)[even]].at[:, piece(q)]
        return remote_copy(landed, landed, second_sem, (p, even, q), c, partner)

    def stats_copy(d):
        return remote_copy(
            stats, stats_all.at[ctx_count - 1 - d], stats_sem, (d - 1,), lax.rem(c + d, ctx_count), e
        )

    def stats_arrived(d):
        landed = stats_all.at[ctx_count - 1 - d]
        return remote_copy(landed, landed, stats_sem, (d - 1,), c, partner)

    loads[0].wait()
    loads[1].wait()
    inputs = states[...].astype(F32)
    inverse = lax.rsqrt(jnp.mean(inputs * inputs, axis=-1, keepdims=True) + EPSILON)
    base[0] = (inputs * inverse * gain[...][None]).astype(BF16)
    base[1] = upstream[...]
    normed = base.at[0]
    expert = lax.broadcasted_iota(jnp.int32, (experts, tokens), 0)
    first, second = ids[0:1, :] == expert, ids[1:2, :] == expert
    chosen = jnp.where(first | second, 1.0, 0.0)
    gate_rows[...] = jnp.where(first, gates[0:1, :], jnp.where(second, gates[1:2, :], 0.0))
    before = jnp.where(
        lax.broadcasted_iota(jnp.int32, (tokens, tokens), 0) < lax.broadcasted_iota(jnp.int32, (tokens, tokens), 1),
        1.0, 0.0,
    ).astype(BF16)
    slots[...] = jnp.where(chosen > 0.5, dot(chosen.astype(BF16), before, 1, 0), -float(4 * tokens))

    def picked(expert_at, count, start):
        number = lax.broadcasted_iota(jnp.int32, (count, tokens), 0) - start
        return jnp.where(slots[pl.ds(expert_at, 1), :] == number.astype(F32), 1.0, 0.0)

    def gathered(expert_at, t, cols):
        chosen_rows = picked(expert_at, capacity, 0)
        gate = jnp.sum(chosen_rows * gate_rows[pl.ds(expert_at, 1), :], axis=1, keepdims=True)
        scale = jnp.where(t == 0, 1.0, gate)
        return (dot(chosen_rows.astype(BF16), base[t, :, cols], 1, 0) * scale).astype(BF16)

    pl.semaphore_wait(barrier, ctx_count + experts - 2)
    for p in remote:
        def run():
            for q in range(pieces):
                outgoing[p - 1, :, piece(q)] = gathered(chip_at(-order[p]) * 2 + near_core, x, piece(q))
                direct_copy(p, q).start()

        if_carrier(p, run)
    for t in range(2):
        to_partner[t] = gathered(partner, t, slice(None))
        partner_copy(t).start()

    loads[2].wait()
    loads[3].wait()

    def first_pass(h, carry):
        cols = head_cols(h)
        scores = dot(keys[:, cols], normed[:, cols], 1, 1) * HEAD ** (-0.5)
        peak = jnp.max(scores, axis=0, keepdims=True)
        weight = jnp.exp(scores - peak)
        slopes = dot(values[:, cols], upstream[:, cols], 1, 1)
        stats[0, pl.ds(h, 1), :] = peak
        stats[1, pl.ds(h, 1), :] = jnp.sum(weight, axis=0, keepdims=True)
        stats[2, pl.ds(h, 1), :] = jnp.sum(weight * slopes, axis=0, keepdims=True)
        return carry

    lax.fori_loop(0, HEADS, first_pass, 0, unroll=4)
    for d in range(1, ctx_count):
        stats_copy(d).start()
    for t in range(2):
        got[t, 0, k] = gathered(e, t, slice(None))

    chunk = 32

    def split(i, carry):
        at = pl.ds(pl.multiple_of(i * chunk, chunk), chunk)
        both = jnp.swapaxes(weights[at], 0, 1)
        w_in[at, :] = both[0]
        w_out[at, :] = both[1]
        return carry

    def second_pass(h, carry):
        cols = head_cols(h)
        key, q, g = keys[:, cols], normed[:, cols], upstream[:, cols]
        scores = dot(key, q, 1, 1) * HEAD ** (-0.5)
        probs = jnp.exp(scores - merged[0, pl.ds(h, 1), :]) / merged[1, pl.ds(h, 1), :]
        slopes = dot(values[:, cols], g, 1, 1)
        score_grad = (probs * (slopes - merged[2, pl.ds(h, 1), :])).astype(BF16)
        values_grad[:, cols] = dot(probs.astype(BF16), g, 1, 0).astype(BF16)
        keys_grad[:, cols] = (dot(score_grad, q, 1, 0) * HEAD ** (-0.5)).astype(BF16)
        query[:, cols] = dot(score_grad, key, 0, 0) * HEAD ** (-0.5)
        return carry

    steps = 4
    quarter = HEADS // steps

    def attend(i):
        lax.fori_loop(i * quarter, (i + 1) * quarter, second_pass, 0, unroll=quarter)

    def merge_stats():
        for d in range(1, ctx_count):
            stats_arrived(d).wait_recv()
        peak = stats[0]
        for d in range(ctx_count - 1):
            peak = jnp.maximum(peak, stats_all[d, 0])
        factor = jnp.exp(stats[0] - peak)
        denominator, inner = stats[1] * factor, stats[2] * factor
        for d in range(ctx_count - 1):
            factor = jnp.exp(stats_all[d, 0] - peak)
            denominator = denominator + stats_all[d, 1] * factor
            inner = inner + stats_all[d, 2] * factor
        merged[0] = peak
        merged[1] = denominator
        merged[2] = inner / denominator

    def forward(p, q):
        def run():
            direct_arrived(p, q).wait_recv()
            if q % 2 == 0:
                full_x_copy(p, q).start()
            for d in range(1, row_count):
                full_y_copy(p, d, q).start()
            if q % 2:
                full_x_copy(p, q).start()

        if_carrier(p, run)

    def forward_again(p, q):
        def run():
            full_arrived(p, 0, q).wait_recv()
            for d in range(1, row_count):
                second_y_copy(p, d, q).start()

        def other():
            full_arrived(p, 2, q).wait_recv()
            second_x_copy(p, 1, q).start()

        if q % 2 == 0:
            if_carrier(p, run)
        else:
            if_carrier(p, lambda: None, other)
            full_arrived(p, 1, q).wait_recv()
            second_x_copy(p, 0, q).start()

    def all_arrived(p):
        for q in range(pieces):
            def run():
                if q % 2:
                    full_arrived(p, 0, q).wait_recv()

            def other():
                if q % 2 == 0:
                    full_arrived(p, 2, q).wait_recv()
                second_arrived(p, 1, q).wait_recv()

            if_carrier(p, run, other)
            if q % 2 == 0:
                full_arrived(p, 1, q).wait_recv()
            second_arrived(p, 0, q).wait_recv()

    def pack(p):
        at = pl.ds(p * pair, pair)
        for t in range(2):
            rows[t, at, :] = got[t, p].reshape(pair, model_width)

    block = min(hidden, 256)
    step = HEAD * math.gcd(tiles, 5)

    def expert(group):
        at = pl.ds(group[0] * pair, len(group) * pair)
        for i in range(hidden // block):
            part = pl.ds(i * block, block)
            pre = dot(rows[0, at, :], w_in[part, :], 1, 1)
            act_grad = dot(rows[1, at, :], w_out[part, :], 1, 1)
            act, slope = gelu_pair(pre)
            activ[at, part] = act.astype(BF16)
            pre_grad[at, part] = (act_grad * slope).astype(BF16)
        for i in range(model_width // step):
            part = pl.ds(i * step, step)
            piece_rows = dot(pre_grad[at, :], w_in[:, part], 1, 0).astype(BF16)
            for n, p in enumerate(group):
                own = piece_rows[n * pair : (n + 1) * pair]
                if p == whole:
                    whole_rows[:, :, part] = own.reshape(2, capacity, step)
                else:
                    partial[pl.ds(p * pair, pair), part] = own

    def share(owner):
        return pl.ds(pl.multiple_of(owner * tiles // ctx_count * HEAD, HEAD), width)

    def near_copy():
        return remote_copy(partial.at[pl.ds(0, pair), :], from_partner, near_sem, (0,), c, partner)

    def part_copy(p, d):
        peer = lax.rem(c + d, ctx_count)
        return remote_copy(
            partial.at[pl.ds(p * pair, pair), share(peer)], parts.at[p - 1, ctx_count - 1 - d],
            part_sem, (p, d - 1), peer, e,
        )

    def part_arrived(p, d):
        landed = parts.at[p - 1, ctx_count - 1 - d]
        return remote_copy(landed, landed, part_sem, (p, d - 1), c, partner)

    def back_position(p):
        return order.index((chips - order[p]) % chips)

    def back_copy(p, core):
        to = chip_at(order[p]) * 2 + core
        at = back_position(p)
        return pltpu.make_async_remote_copy(
            src_ref=reduced.at[p - 1, core], dst_ref=returned.at[at - 1, k],
            send_sem=back_sem.at[0, p, core], recv_sem=back_sem.at[1, at, k],
            device_id={"ctx": c, "exp": to}, device_id_type=MESH,
        )

    def back_arrived(p, core):
        landed = returned.at[p - 1, core]
        return remote_copy(landed, landed, back_sem, (p, core), c, partner)

    def whole_copy(core):
        to = chip_at(order[whole]) * 2 + core
        return pltpu.make_async_remote_copy(
            src_ref=whole_rows.at[core], dst_ref=whole_got.at[k],
            send_sem=whole_sem.at[0, core], recv_sem=whole_sem.at[1, k],
            device_id={"ctx": c, "exp": to}, device_id_type=MESH,
        )

    def whole_arrived(core):
        landed = whole_got.at[core]
        return remote_copy(landed, landed, whole_sem, (core,), c, partner)

    row_half = tokens // 2
    row_halves = (pl.ds(0, row_half), pl.ds(row_half, tokens - row_half))

    def local_copy(d, r):
        peer = lax.rem(c + d, ctx_count)
        return remote_copy(
            local_total.at[row_halves[r], share(peer)], local_parts.at[ctx_count - 1 - d, row_halves[r]],
            local_sem, (d - 1, r), peer, e,
        )

    def local_arrived(d, r):
        landed = local_parts.at[ctx_count - 1 - d, row_halves[r]]
        return remote_copy(landed, landed, local_sem, (d - 1, r), c, partner)

    def final_copy(kind, d, r):
        owner = c if kind < 2 else (x_peer if kind == 2 else row_peer(d))
        to = x_peer if kind in (0, 3) else row_peer(d)
        back = 0 if kind == 0 else d if kind == 3 else row_count - d
        block = finals.at[owner, row_halves[r]]
        return remote_copy(block, block, final_sem, (kind, d, r), to, e, (kind, back, r))

    def final_arrived(kind, d, r):
        owner = x_peer if kind == 0 else row_peer(d)
        if kind > 1:
            owner = lax.rem(y + d, row_count) * 2 + (1 - x)
        landed = finals.at[owner, row_halves[r]]
        return remote_copy(landed, landed, final_sem, (kind, d, r), c, partner)

    far_first = sorted(range(1, ctx_count), key=lambda d: d != ctx_count // 2)

    def send_parts(p):
        for d in far_first:
            part_copy(p, d).start()

    def reduce_parts(p):
        summed = partial[pl.ds(p * pair, pair), share(c)].astype(F32)
        for d in far_first:
            part_arrived(p, d).wait_recv()
        for d in range(ctx_count - 1):
            summed = summed + parts[p - 1, d].astype(F32)
        reduced[p - 1] = summed.astype(BF16).reshape(2, capacity, width)
        for core in range(2):
            back_copy(p, core).start()

    def near_total():
        near_copy().wait_recv()
        for i in range(model_width // step):
            part = pl.ds(i * step, step)
            query[:, part] += dot(select_near[0], partial[pl.ds(0, pair), part], 0, 0) + dot(
                select_near[1], from_partner[:, part], 0, 0
            )

    def whole_total():
        for core in range(2):
            whole_arrived(core).wait_recv()
        for i in range(model_width // step):
            part = pl.ds(i * step, step)
            summed = query[:, part]
            for core in range(2):
                summed += dot(select[back_position(whole) - 1, core], whole_got[core, :, part], 0, 0)
            local_total[:, part] = summed.astype(BF16)

    def send_total(r):
        for d in far_first:
            local_copy(d, r).start()

    def split_weights():
        loads[4].wait()
        lax.fori_loop(0, hidden // chunk, split, 0)

    def first_attend():
        merge_stats()
        attend(0)

    def last_attend():
        attend(steps - 1)
        for i in range(2):
            select_near[i] = picked((e, partner)[i], pair, k * capacity).astype(BF16)
        for p in remote:
            for core in range(2):
                select[p - 1, core] = picked(chip_at(order[p]) * 2 + core, capacity, 0).astype(BF16)
        for t in range(2):
            partner_arrived(t).wait_recv()
        pack(0)

    def run_group(group):
        for p in group:
            if p:
                all_arrived(p)
                pack(p)
        if group is groups[-1]:
            pass
        expert(group)
        for p in group:
            if p == whole:
                for core in range(2):
                    whole_copy(core).start()
            elif p:
                send_parts(p)
            else:
                near_copy().start()
        if group is groups[-1]:
            near_total()
            whole_total()
            send_total(0)
            send_total(1)
        for p in pending:
            reduce_parts(p)
        pending[:] = [p for p in group if p and p != whole]

    pending = []
    moves = [(p, q) for p in remote for q in range(pieces)]
    pace, again, ready = 2.5 / pieces, 1.8, 4.6
    plan = [(n * pace, functools.partial(forward, *move)) for n, move in enumerate(moves)]
    plan += [(n * pace + again, functools.partial(forward_again, *move)) for n, move in enumerate(moves)]
    plan += [
        (moves.index((group[-1], pieces - 1)) * pace + ready, functools.partial(run_group, group)) for group in groups
    ]
    work = [split_weights, first_attend] + [functools.partial(attend, i) for i in range(1, steps - 1)] + [last_attend]
    plan += list(zip((0.1, 1.3, 1.9, 2.6, 3.8), work))
    for _, action in sorted(plan, key=lambda item: item[0]):
        action()
    for p in pending:
        reduce_parts(p)
    for d in far_first:
        for r in range(2):
            local_arrived(d, r).wait_recv()
    summed = local_total[:, share(c)].astype(F32)
    for d in range(ctx_count - 1):
        summed = summed + local_parts[d].astype(F32)
    for p in sorted(set(remote) - {back_position(whole)}, key=back_position):
        for core in range(2):
            back_arrived(p, core).wait_recv()
            summed = summed + dot(select[p - 1, core], returned[p - 1, core], 0, 0)
    finals[c] = summed.astype(BF16)
    along = range(1, row_count)
    gathers = [(0, 0, 0)] + [(1, d, 1) for d in along] + [(0, 0, 1)] + [(1, d, 0) for d in along]
    gathers_again = [(2, d, 0) for d in along] + [(3, d, 1) for d in along]
    for move in gathers:
        final_copy(*move).start()
    final_arrived(0, 0, 0).wait_recv()
    for d in along:
        final_copy(2, d, 0).start()
    for d in along:
        final_arrived(1, d, 1).wait_recv()
        final_copy(3, d, 1).start()
    final_arrived(0, 0, 1).wait_recv()
    for d in along:
        final_arrived(1, d, 0).wait_recv()
        final_arrived(2, d, 0).wait_recv()
        final_arrived(3, d, 1).wait_recv()
    for owner in range(ctx_count):
        total[:, pl.ds(owner * tiles // ctx_count * HEAD, width)] = finals[owner]
    lines = 32

    def norm_gradient(i, carry):
        at = pl.ds(pl.multiple_of(i * lines, lines), lines)
        values_in = states[at, :].astype(F32)
        scale = lax.rsqrt(jnp.mean(values_in * values_in, axis=-1, keepdims=True) + EPSILON)
        unit = values_in * scale
        scaled = total[at, :].astype(F32) * gain[...][None]
        states_grad[at, :] = (
            upstream[at, :].astype(F32) + scale * (scaled - unit * jnp.mean(scaled * unit, axis=-1, keepdims=True))
        ).astype(BF16)
        return carry

    lax.fori_loop(0, tokens // lines, norm_gradient, 0)

    for t in range(2):
        partner_copy(t).wait_send()
    near_copy().wait_send()
    for d in range(1, ctx_count):
        stats_copy(d).wait_send()
        for r in range(2):
            local_copy(d, r).wait_send()
    for kind, d, r in gathers + gathers_again:
        final_copy(kind, d, r).wait_send()
    for p in remote:
        def run():
            for q in range(pieces):
                direct_copy(p, q).wait_send()
                full_x_copy(p, q).wait_send()
                for d in range(1, row_count):
                    full_y_copy(p, d, q).wait_send()
                    if q % 2 == 0:
                        second_y_copy(p, d, q).wait_send()

        def other():
            for q in range(1, pieces, 2):
                second_x_copy(p, 1, q).wait_send()

        if_carrier(p, run, other)
        for q in range(1, pieces, 2):
            second_x_copy(p, 0, q).wait_send()
        for core in range(2):
            (whole_copy(core) if p == whole else back_copy(p, core)).wait_send()
        for d in range(1, ctx_count):
            if p != whole:
                part_copy(p, d).wait_send()


def weights_kernel(
    pre_grad, activ, rows, states_grad, keys_grad, values_grad,
    weights_out, states_out, keys_out, values_out, grad, grad_sem, pass_sem,
):
    passed = [
        pltpu.make_async_copy(source, target, pass_sem.at[n])
        for n, (source, target) in enumerate(
            ((states_grad, states_out), (keys_grad, keys_out), (values_grad, values_out))
        )
    ]
    for copy in passed:
        copy.start()
    hidden = grad.shape[0]
    block = min(hidden, 128)

    def store(i):
        at = pl.ds(i * block, block)
        return pltpu.make_async_copy(grad.at[at], weights_out.at[at], grad_sem.at[i])

    for i in range(hidden // block):
        at = pl.ds(i * block, block)
        grad[at, 0, :] = dot(pre_grad[:, at], rows[0], 0, 0).astype(BF16)
        grad[at, 1, :] = dot(activ[:, at], rows[1], 0, 0).astype(BF16)
        store(i).start()
    for i in range(hidden // block):
        store(i).wait()
    for copy in passed:
        copy.wait()


def on_device(
    states, out_grad, doc_keys, doc_values, norm_gain, expert_ids, gate_values, expert_weights
):
    tokens, model_width = states.shape[1:]
    key_count = doc_keys.shape[1]
    ctx_count, experts = lax.axis_size("ctx"), lax.axis_size("exp")
    chips = experts // 2
    hidden = expert_weights.shape[1]
    capacity = 8 * -(-5 * TOP * tokens // (32 * experts))
    pair = 2 * capacity
    slot_rows = experts * capacity
    tiles = model_width // HEAD
    width = HEAD * max(-(-(c + 1) * tiles // ctx_count) - c * tiles // ctx_count for c in range(ctx_count))
    order = [0] + sorted(range(1, chips), key=lambda j: min(j, chips - j))
    pieces = 2
    groups = [[0, 1]] + [[p] for p in range(2, chips)]
    vmem = pl.BlockSpec(memory_space=pltpu.VMEM)
    hbm = pl.BlockSpec(memory_space=pltpu.HBM)
    shape = jax.ShapeDtypeStruct
    dma = pltpu.SemaphoreType.DMA
    near = max(chips - 1, 1)
    scratch = [
        ((tokens, model_width), BF16),
        ((tokens, model_width), BF16),
        ((key_count, model_width), BF16),
        ((key_count, model_width), BF16),
        ((hidden, 2, model_width), BF16),
        ((hidden, model_width), BF16),
        ((hidden, model_width), BF16),
        ((2, tokens, model_width), BF16),
        ((experts, tokens), F32),
        ((experts, tokens), F32),
        ((near, capacity, model_width), BF16),
        ((2, capacity, model_width), BF16),
        ((2, chips, 2, capacity, model_width), BF16),
        ((slot_rows, model_width), BF16),
        ((2, capacity, model_width), BF16),
        ((2, capacity, model_width), BF16),
        ((pair, model_width), BF16),
        ((near, 2, capacity, tokens), BF16),
        ((2, pair, tokens), BF16),
        ((tokens, model_width), F32),
        ((tokens, model_width), BF16),
        ((3, HEADS, tokens), F32),
        ((ctx_count - 1, 3, HEADS, tokens), F32),
        ((3, HEADS, tokens), F32),
        ((near, ctx_count - 1, pair, width), BF16),
        ((near, 2, capacity, width), BF16),
        ((near, 2, capacity, width), BF16),
        ((ctx_count - 1, tokens, width), BF16),
        ((ctx_count, tokens, width), BF16),
        ((tokens, model_width), BF16),
    ]
    semaphores = [
        (5,),
        (2, chips, pieces),
        (2, 2),
        (2, chips, max(ctx_count // 2, 3), pieces),
        (2, chips, ctx_count // 2 + 1, pieces),
        (2, ctx_count - 1),
        (2, 1),
        (2, 2),
        (2, chips, ctx_count - 1),
        (2, chips, 2),
        (2, ctx_count - 1, 2),
        (2, 4, ctx_count // 2, 2),
    ]
    rows, pre_grad, activ, keys_grad, values_grad, states_grad = pl.pallas_call(
        functools.partial(block_kernel, ctx_count, experts, order, groups, pieces, 1),
        out_shape=(
            shape((2, slot_rows, model_width), BF16),
            shape((slot_rows, hidden), BF16),
            shape((slot_rows, hidden), BF16),
            shape((key_count, model_width), BF16),
            shape((key_count, model_width), BF16),
            shape((tokens, model_width), BF16),
        ),
        in_specs=[vmem] * 3 + [hbm] * 5,
        out_specs=(vmem,) * 6,
        scratch_shapes=[pltpu.VMEM(s, t) for s, t in scratch] + [dma(s) for s in semaphores],
        compiler_params=pltpu.CompilerParams(
            vmem_limit_bytes=VMEM_LIMIT, collective_id=0, has_side_effects=True
        ),
    )(
        *(pltpu.with_memory_space_constraint(a, pltpu.HBM) for a in (norm_gain, expert_ids[0].T, gate_values[0].T)),
        *(pltpu.with_memory_space_constraint(a, pltpu.HBM) for a in (states[0], out_grad[0], doc_keys[0], doc_values[0], expert_weights[0])),
    )
    weights_grad, states_grad, keys_grad, values_grad = pl.pallas_call(
        weights_kernel,
        out_shape=(
            shape((hidden, 2, model_width), BF16),
            shape((tokens, model_width), BF16),
            shape((key_count, model_width), BF16),
            shape((key_count, model_width), BF16),
        ),
        in_specs=[vmem] * 6,
        out_specs=(hbm,) * 4,
        scratch_shapes=[
            pltpu.VMEM((hidden, 2, model_width), BF16),
            dma((-(-hidden // 128),)),
            dma((3,)),
        ],
        compiler_params=pltpu.CompilerParams(vmem_limit_bytes=SECOND_LIMIT),
    )(pre_grad, activ, rows, states_grad, keys_grad, values_grad)
    return states_grad[None], keys_grad[None], values_grad[None], weights_grad[None]


def solution(mesh):
    return jax.shard_map(
        on_device,
        mesh=mesh,
        in_specs=(
            P("exp", None, None),
            P("exp", None, None),
            P("exp", "ctx", None),
            P("exp", "ctx", None),
            P(),
            P("exp", None, None),
            P("exp", None, None),
            P("exp", "ctx", None, None),
        ),
        out_specs=(
            P("exp", None, None),
            P("exp", "ctx", None),
            P("exp", "ctx", None),
            P("exp", "ctx", None, None),
        ),
        check_vma=False,
    )
```

```python
import functools
import math
import jax
import jax.numpy as jnp
from jax import lax
from jax.experimental import pallas as pl
from jax.experimental.pallas import tpu as pltpu
from jax.sharding import PartitionSpec as P

HEADS = 20
HEAD = 128
TOP = 2


EPSILON = 1e-05
MESH = pl.DeviceIdType.MESH
F32 = jnp.float32
BF16 = jnp.bfloat16
VMEM_LIMIT = 44 * 1024 * 1024
SECOND_LIMIT = 24 * 1024 * 1024


def dot(a, b, ca, cb):
    return lax.dot_general(a, b, (((ca,), (cb,)), ((), ())), preferred_element_type=F32)


def head_cols(h):
    return pl.ds(pl.multiple_of(h * HEAD, HEAD), HEAD)


def gelu_pair(v):
    slope, cubic = math.sqrt(2.0 / math.pi), 0.044715
    square = v * v
    tanh = jnp.tanh(slope * v * (1.0 + cubic * square))
    half = 0.5 * (1.0 + tanh)
    inner = slope * (1.0 + 3.0 * cubic * square)
    return v * half, half + 0.5 * v * (1.0 - tanh * tanh) * inner


def block_kernel(
    ctx_count, experts, order, groups, pieces, whole,
    gain, ids, gates, states_hbm, upstream_hbm, keys_hbm, values_hbm, weights_hbm,
    weights_grad, keys_grad, values_grad, states_grad,
    rows, pre_grad, activ, states, upstream, keys, values, weights, w_in, w_out, base, slots, gate_rows, outgoing, to_partner,
    got, partial, whole_rows, whole_got, from_partner, select, select_near, query, local_total,
    stats, stats_all, merged,
    parts, reduced, returned, local_parts, finals, total,
    load_sem, direct_sem, partner_sem, full_sem, second_sem, stats_sem,
    near_sem, whole_sem, part_sem, back_sem, local_sem, final_sem,
):
    c, e = lax.axis_index("ctx"), lax.axis_index("exp")
    chips = experts // 2
    tokens, model_width = states.shape
    capacity = got.shape[3]
    hidden = w_in.shape[0]
    pair = 2 * capacity
    width = finals.shape[2]
    tiles = model_width // HEAD
    row_count = ctx_count // 2
    sets = row_count // 2
    x, y = lax.rem(c, 2), c // 2
    z, k = e // 2, lax.rem(e, 2)
    remote = range(1, chips)
    x_peer, partner = y * 2 + (1 - x), z * 2 + (1 - k)
    near_core, far_core = lax.rem(k + y, 2), lax.rem(k + 1 + y, 2)

    def chip_at(offset):
        return lax.rem(z + offset + chips, chips)

    def row_peer(d):
        return lax.rem(y + d, row_count) * 2 + x

    def if_carrier(p, run, other=None):
        if sets == 1:
            run()
        else:
            carrier = y // 2 == p % sets
            pl.when(carrier)(run)
            if other is not None:
                pl.when(jnp.logical_not(carrier))(other)

    def remote_copy(src, dst, sem, at, to_c, to_e, got_at=None):
        return pltpu.make_async_remote_copy(
            src_ref=src, dst_ref=dst,
            send_sem=sem.at[(0, *at)], recv_sem=sem.at[(1, *(at if got_at is None else got_at))],
            device_id={"ctx": to_c, "exp": to_e}, device_id_type=MESH,
        )

    loads = [
        pltpu.make_async_copy(source, target, load_sem.at[n])
        for n, (source, target) in enumerate((
            (states_hbm, states), (upstream_hbm, upstream), (keys_hbm, keys),
            (values_hbm, values), (weights_hbm, weights),
        ))
    ]
    for load in loads:
        load.start()

    barrier = pltpu.get_barrier_semaphore()
    for d in range(1, ctx_count):
        pl.semaphore_signal(barrier, inc=1, device_id={"ctx": lax.rem(c + d, ctx_count), "exp": e}, device_id_type=MESH)
    for d in range(1, experts):
        pl.semaphore_signal(barrier, inc=1, device_id={"ctx": c, "exp": lax.rem(e + d, experts)}, device_id_type=MESH)

    def piece(q):
        start, end = (at * tiles // pieces * HEAD for at in (q, q + 1))
        return pl.ds(start, end - start)

    def direct_copy(p, q):
        to = chip_at(-order[p]) * 2 + near_core
        return remote_copy(
            outgoing.at[p - 1, :, piece(q)], got.at[x, p, k].at[:, piece(q)], direct_sem, (p, q), c, to
        )

    def direct_arrived(p, q):
        landed = got.at[x, p, near_core].at[:, piece(q)]
        return remote_copy(landed, landed, direct_sem, (p, q), c, partner)

    def partner_copy(t):
        return remote_copy(to_partner.at[t], got.at[t, 0, k], partner_sem, (t,), c, partner)

    def partner_arrived(t):
        landed = got.at[t, 0, 1 - k]
        return remote_copy(landed, landed, partner_sem, (t,), c, partner)

    def full_x_copy(p, q):
        block = got.at[x, p, near_core].at[:, piece(q)]
        return remote_copy(block, block, full_sem, (p, 0, q), x_peer, e)

    def full_y_copy(p, d, q):
        block = got.at[x, p, near_core].at[:, piece(q)]
        return remote_copy(block, block, full_sem, (p, d, q), row_peer(d), e, (p, 2 - d % 2, q))

    def full_block(p, way, q):
        block = (got.at[1 - x, p, near_core], got.at[x, p, far_core], got.at[x, p, near_core])[way]
        return block.at[:, piece(q)]

    def full_arrived(p, way, q):
        landed = full_block(p, way, q)
        return remote_copy(landed, landed, full_sem, (p, way, q), c, partner)

    def second_y_copy(p, d, q):
        block = got.at[1 - x, p, near_core].at[:, piece(q)]
        return remote_copy(block, block, second_sem, (p, d + 1, q), row_peer(d), e, (p, 1 - d % 2, q))

    def second_x_copy(p, even, q):
        block = full_block(p, 1 + even, q)
        return remote_copy(block, block, second_sem, (p, even, q), x_peer, e)

    def second_arrived(p, even, q):
        landed = got.at[1 - x, p, (far_core, near_core)[even]].at[:, piece(q)]
        return remote_copy(landed, landed, second_sem, (p, even, q), c, partner)

    def stats_copy(d):
        return remote_copy(
            stats, stats_all.at[ctx_count - 1 - d], stats_sem, (d - 1,), lax.rem(c + d, ctx_count), e
        )

    def stats_arrived(d):
        landed = stats_all.at[ctx_count - 1 - d]
        return remote_copy(landed, landed, stats_sem, (d - 1,), c, partner)

    loads[0].wait()
    loads[1].wait()
    inputs = states[...].astype(F32)
    inverse = lax.rsqrt(jnp.mean(inputs * inputs, axis=-1, keepdims=True) + EPSILON)
    base[0] = (inputs * inverse * gain[...][None]).astype(BF16)
    base[1] = upstream[...]
    normed = base.at[0]
    expert = lax.broadcasted_iota(jnp.int32, (experts, tokens), 0)
    first, second = ids[0:1, :] == expert, ids[1:2, :] == expert
    chosen = jnp.where(first | second, 1.0, 0.0)
    gate_rows[...] = jnp.where(first, gates[0:1, :], jnp.where(second, gates[1:2, :], 0.0))
    before = jnp.where(
        lax.broadcasted_iota(jnp.int32, (tokens, tokens), 0) < lax.broadcasted_iota(jnp.int32, (tokens, tokens), 1),
        1.0, 0.0,
    ).astype(BF16)
    slots[...] = jnp.where(chosen > 0.5, dot(chosen.astype(BF16), before, 1, 0), -float(4 * tokens))

    def picked(expert_at, count, start):
        number = lax.broadcasted_iota(jnp.int32, (count, tokens), 0) - start
        return jnp.where(slots[pl.ds(expert_at, 1), :] == number.astype(F32), 1.0, 0.0)

    def gathered(expert_at, t, cols):
        chosen_rows = picked(expert_at, capacity, 0)
        gate = jnp.sum(chosen_rows * gate_rows[pl.ds(expert_at, 1), :], axis=1, keepdims=True)
        scale = jnp.where(t == 0, 1.0, gate)
        return (dot(chosen_rows.astype(BF16), base[t, :, cols], 1, 0) * scale).astype(BF16)

    pl.semaphore_wait(barrier, ctx_count + experts - 2)
    for p in remote:
        def run():
            for q in range(pieces):
                outgoing[p - 1, :, piece(q)] = gathered(chip_at(-order[p]) * 2 + near_core, x, piece(q))
                direct_copy(p, q).start()

        if_carrier(p, run)
    for t in range(2):
        to_partner[t] = gathered(partner, t, slice(None))
        partner_copy(t).start()

    loads[2].wait()
    loads[3].wait()

    def first_pass(h, carry):
        cols = head_cols(h)
        scores = dot(keys[:, cols], normed[:, cols], 1, 1) * HEAD ** (-0.5)
        peak = jnp.max(scores, axis=0, keepdims=True)
        weight = jnp.exp(scores - peak)
        slopes = dot(values[:, cols], upstream[:, cols], 1, 1)
        stats[0, pl.ds(h, 1), :] = peak
        stats[1, pl.ds(h, 1), :] = jnp.sum(weight, axis=0, keepdims=True)
        stats[2, pl.ds(h, 1), :] = jnp.sum(weight * slopes, axis=0, keepdims=True)
        return carry

    lax.fori_loop(0, HEADS, first_pass, 0, unroll=4)
    for d in range(1, ctx_count):
        stats_copy(d).start()
    for t in range(2):
        got[t, 0, k] = gathered(e, t, slice(None))

    chunk = 32

    def split(i, carry):
        at = pl.ds(pl.multiple_of(i * chunk, chunk), chunk)
        both = jnp.swapaxes(weights[at], 0, 1)
        w_in[at, :] = both[0]
        w_out[at, :] = both[1]
        return carry

    def second_pass(h, carry):
        cols = head_cols(h)
        key, q, g = keys[:, cols], normed[:, cols], upstream[:, cols]
        scores = dot(key, q, 1, 1) * HEAD ** (-0.5)
        probs = jnp.exp(scores - merged[0, pl.ds(h, 1), :]) / merged[1, pl.ds(h, 1), :]
        slopes = dot(values[:, cols], g, 1, 1)
        score_grad = (probs * (slopes - merged[2, pl.ds(h, 1), :])).astype(BF16)
        values_grad[:, cols] = dot(probs.astype(BF16), g, 1, 0).astype(BF16)
        keys_grad[:, cols] = (dot(score_grad, q, 1, 0) * HEAD ** (-0.5)).astype(BF16)
        query[:, cols] = dot(score_grad, key, 0, 0) * HEAD ** (-0.5)
        return carry

    steps = 4
    quarter = HEADS // steps

    def attend(i):
        lax.fori_loop(i * quarter, (i + 1) * quarter, second_pass, 0, unroll=quarter)

    def merge_stats():
        for d in range(1, ctx_count):
            stats_arrived(d).wait_recv()
        peak = stats[0]
        for d in range(ctx_count - 1):
            peak = jnp.maximum(peak, stats_all[d, 0])
        factor = jnp.exp(stats[0] - peak)
        denominator, inner = stats[1] * factor, stats[2] * factor
        for d in range(ctx_count - 1):
            factor = jnp.exp(stats_all[d, 0] - peak)
            denominator = denominator + stats_all[d, 1] * factor
            inner = inner + stats_all[d, 2] * factor
        merged[0] = peak
        merged[1] = denominator
        merged[2] = inner / denominator

    def forward(p, q):
        def run():
            direct_arrived(p, q).wait_recv()
            if q % 2 == 0:
                full_x_copy(p, q).start()
            for d in range(1, row_count):
                full_y_copy(p, d, q).start()
            if q % 2:
                full_x_copy(p, q).start()

        if_carrier(p, run)

    def forward_again(p, q):
        def run():
            full_arrived(p, 0, q).wait_recv()
            for d in range(1, row_count):
                second_y_copy(p, d, q).start()

        def other():
            full_arrived(p, 2, q).wait_recv()
            second_x_copy(p, 1, q).start()

        if q % 2 == 0:
            if_carrier(p, run)
        else:
            if_carrier(p, lambda: None, other)
            full_arrived(p, 1, q).wait_recv()
            second_x_copy(p, 0, q).start()

    def all_arrived(p):
        for q in range(pieces):
            def run():
                if q % 2:
                    full_arrived(p, 0, q).wait_recv()

            def other():
                if q % 2 == 0:
                    full_arrived(p, 2, q).wait_recv()
                second_arrived(p, 1, q).wait_recv()

            if_carrier(p, run, other)
            if q % 2 == 0:
                full_arrived(p, 1, q).wait_recv()
            second_arrived(p, 0, q).wait_recv()

    def pack(p):
        at = pl.ds(p * pair, pair)
        for t in range(2):
            rows[t, at, :] = got[t, p].reshape(pair, model_width)

    block = min(hidden, 256)
    step = HEAD * math.gcd(tiles, 5)

    def expert(group):
        at = pl.ds(group[0] * pair, len(group) * pair)
        for i in range(hidden // block):
            part = pl.ds(i * block, block)
            pre = dot(rows[0, at, :], w_in[part, :], 1, 1)
            act_grad = dot(rows[1, at, :], w_out[part, :], 1, 1)
            act, slope = gelu_pair(pre)
            activ[at, part] = act.astype(BF16)
            pre_grad[at, part] = (act_grad * slope).astype(BF16)
        for i in range(model_width // step):
            part = pl.ds(i * step, step)
            piece_rows = dot(pre_grad[at, :], w_in[:, part], 1, 0).astype(BF16)
            for n, p in enumerate(group):
                own = piece_rows[n * pair : (n + 1) * pair]
                if p == whole:
                    whole_rows[:, :, part] = own.reshape(2, capacity, step)
                else:
                    partial[pl.ds(p * pair, pair), part] = own

    def share(owner):
        return pl.ds(pl.multiple_of(owner * tiles // ctx_count * HEAD, HEAD), width)

    def near_copy():
        return remote_copy(partial.at[pl.ds(0, pair), :], from_partner, near_sem, (0,), c, partner)

    def part_copy(p, d):
        peer = lax.rem(c + d, ctx_count)
        return remote_copy(
            partial.at[pl.ds(p * pair, pair), share(peer)], parts.at[p - 1, ctx_count - 1 - d],
            part_sem, (p, d - 1), peer, e,
        )

    def part_arrived(p, d):
        landed = parts.at[p - 1, ctx_count - 1 - d]
        return remote_copy(landed, landed, part_sem, (p, d - 1), c, partner)

    def back_position(p):
        return order.index((chips - order[p]) % chips)

    def back_copy(p, core):
        to = chip_at(order[p]) * 2 + core
        at = back_position(p)
        return pltpu.make_async_remote_copy(
            src_ref=reduced.at[p - 1, core], dst_ref=returned.at[at - 1, k],
            send_sem=back_sem.at[0, p, core], recv_sem=back_sem.at[1, at, k],
            device_id={"ctx": c, "exp": to}, device_id_type=MESH,
        )

    def back_arrived(p, core):
        landed = returned.at[p - 1, core]
        return remote_copy(landed, landed, back_sem, (p, core), c, partner)

    def whole_copy(core):
        to = chip_at(order[whole]) * 2 + core
        return pltpu.make_async_remote_copy(
            src_ref=whole_rows.at[core], dst_ref=whole_got.at[k],
            send_sem=whole_sem.at[0, core], recv_sem=whole_sem.at[1, k],
            device_id={"ctx": c, "exp": to}, device_id_type=MESH,
        )

    def whole_arrived(core):
        landed = whole_got.at[core]
        return remote_copy(landed, landed, whole_sem, (core,), c, partner)

    row_half = tokens // 2
    row_halves = (pl.ds(0, row_half), pl.ds(row_half, tokens - row_half))

    def local_copy(d, r):
        peer = lax.rem(c + d, ctx_count)
        return remote_copy(
            local_total.at[row_halves[r], share(peer)], local_parts.at[ctx_count - 1 - d, row_halves[r]],
            local_sem, (d - 1, r), peer, e,
        )

    def local_arrived(d, r):
        landed = local_parts.at[ctx_count - 1 - d, row_halves[r]]
        return remote_copy(landed, landed, local_sem, (d - 1, r), c, partner)

    def final_copy(kind, d, r):
        owner = c if kind < 2 else (x_peer if kind == 2 else row_peer(d))
        to = x_peer if kind in (0, 3) else row_peer(d)
        back = 0 if kind == 0 else d if kind == 3 else row_count - d
        block = finals.at[owner, row_halves[r]]
        return remote_copy(block, block, final_sem, (kind, d, r), to, e, (kind, back, r))

    def final_arrived(kind, d, r):
        owner = x_peer if kind == 0 else row_peer(d)
        if kind > 1:
            owner = lax.rem(y + d, row_count) * 2 + (1 - x)
        landed = finals.at[owner, row_halves[r]]
        return remote_copy(landed, landed, final_sem, (kind, d, r), c, partner)

    far_first = sorted(range(1, ctx_count), key=lambda d: d != ctx_count // 2)

    def send_parts(p):
        for d in far_first:
            part_copy(p, d).start()

    def reduce_parts(p):
        summed = partial[pl.ds(p * pair, pair), share(c)].astype(F32)
        for d in far_first:
            part_arrived(p, d).wait_recv()
        for d in range(ctx_count - 1):
            summed = summed + parts[p - 1, d].astype(F32)
        reduced[p - 1] = summed.astype(BF16).reshape(2, capacity, width)
        for core in range(2):
            back_copy(p, core).start()

    def near_total():
        near_copy().wait_recv()
        for i in range(model_width // step):
            part = pl.ds(i * step, step)
            query[:, part] += dot(select_near[0], partial[pl.ds(0, pair), part], 0, 0) + dot(
                select_near[1], from_partner[:, part], 0, 0
            )

    def whole_total():
        for core in range(2):
            whole_arrived(core).wait_recv()
        for i in range(model_width // step):
            part = pl.ds(i * step, step)
            summed = query[:, part]
            for core in range(2):
                summed += dot(select[back_position(whole) - 1, core], whole_got[core, :, part], 0, 0)
            local_total[:, part] = summed.astype(BF16)

    def send_total(r):
        for d in far_first:
            local_copy(d, r).start()

    def split_weights():
        loads[4].wait()
        lax.fori_loop(0, hidden // chunk, split, 0)

    def first_attend():
        merge_stats()
        attend(0)

    def last_attend():
        attend(steps - 1)
        for i in range(2):
            select_near[i] = picked((e, partner)[i], pair, k * capacity).astype(BF16)
        for p in remote:
            for core in range(2):
                select[p - 1, core] = picked(chip_at(order[p]) * 2 + core, capacity, 0).astype(BF16)
        for t in range(2):
            partner_arrived(t).wait_recv()
        pack(0)

    def run_group(group):
        for p in group:
            if p:
                all_arrived(p)
                pack(p)
        if group is groups[-1]:
            pass
        expert(group)
        for p in group:
            if p == whole:
                for core in range(2):
                    whole_copy(core).start()
            elif p:
                send_parts(p)
            else:
                near_copy().start()
        if group is groups[-1]:
            near_total()
            whole_total()
            send_total(0)
            send_total(1)
        for p in pending:
            reduce_parts(p)
        pending[:] = [p for p in group if p and p != whole]

    pending = []
    moves = [(p, q) for p in remote for q in range(pieces)]
    pace, again, ready = 2.5 / pieces, 1.8, 4.6
    plan = [(n * pace, functools.partial(forward, *move)) for n, move in enumerate(moves)]
    plan += [(n * pace + again, functools.partial(forward_again, *move)) for n, move in enumerate(moves)]
    plan += [
        (moves.index((group[-1], pieces - 1)) * pace + ready, functools.partial(run_group, group)) for group in groups
    ]
    work = [split_weights, first_attend] + [functools.partial(attend, i) for i in range(1, steps - 1)] + [last_attend]
    plan += list(zip((0.1, 1.3, 1.9, 2.6, 3.8), work))
    for _, action in sorted(plan, key=lambda item: item[0]):
        action()
    for p in pending:
        reduce_parts(p)
    strip = min(hidden, 128)
    for i in range(hidden // strip):
        at = pl.ds(i * strip, strip)
        weights_grad[at, 0, :] = dot(pre_grad[:, at], rows[0], 0, 0).astype(BF16)
        weights_grad[at, 1, :] = dot(activ[:, at], rows[1], 0, 0).astype(BF16)
    for d in far_first:
        for r in range(2):
            local_arrived(d, r).wait_recv()
    summed = local_total[:, share(c)].astype(F32)
    for d in range(ctx_count - 1):
        summed = summed + local_parts[d].astype(F32)
    for p in sorted(set(remote) - {back_position(whole)}, key=back_position):
        for core in range(2):
            back_arrived(p, core).wait_recv()
            summed = summed + dot(select[p - 1, core], returned[p - 1, core], 0, 0)
    finals[c] = summed.astype(BF16)
    along = range(1, row_count)
    gathers = [(0, 0, 0)] + [(1, d, 1) for d in along] + [(0, 0, 1)] + [(1, d, 0) for d in along]
    gathers_again = [(2, d, 0) for d in along] + [(3, d, 1) for d in along]
    for move in gathers:
        final_copy(*move).start()
    final_arrived(0, 0, 0).wait_recv()
    for d in along:
        final_copy(2, d, 0).start()
    for d in along:
        final_arrived(1, d, 1).wait_recv()
        final_copy(3, d, 1).start()
    final_arrived(0, 0, 1).wait_recv()
    for d in along:
        final_arrived(1, d, 0).wait_recv()
        final_arrived(2, d, 0).wait_recv()
        final_arrived(3, d, 1).wait_recv()
    for owner in range(ctx_count):
        total[:, pl.ds(owner * tiles // ctx_count * HEAD, width)] = finals[owner]
    lines = 32

    def norm_gradient(i, carry):
        at = pl.ds(pl.multiple_of(i * lines, lines), lines)
        values_in = states[at, :].astype(F32)
        scale = lax.rsqrt(jnp.mean(values_in * values_in, axis=-1, keepdims=True) + EPSILON)
        unit = values_in * scale
        scaled = total[at, :].astype(F32) * gain[...][None]
        states_grad[at, :] = (
            upstream[at, :].astype(F32) + scale * (scaled - unit * jnp.mean(scaled * unit, axis=-1, keepdims=True))
        ).astype(BF16)
        return carry

    lax.fori_loop(0, tokens // lines, norm_gradient, 0)

    for t in range(2):
        partner_copy(t).wait_send()
    near_copy().wait_send()
    for d in range(1, ctx_count):
        stats_copy(d).wait_send()
        for r in range(2):
            local_copy(d, r).wait_send()
    for kind, d, r in gathers + gathers_again:
        final_copy(kind, d, r).wait_send()
    for p in remote:
        def run():
            for q in range(pieces):
                direct_copy(p, q).wait_send()
                full_x_copy(p, q).wait_send()
                for d in range(1, row_count):
                    full_y_copy(p, d, q).wait_send()
                    if q % 2 == 0:
                        second_y_copy(p, d, q).wait_send()

        def other():
            for q in range(1, pieces, 2):
                second_x_copy(p, 1, q).wait_send()

        if_carrier(p, run, other)
        for q in range(1, pieces, 2):
            second_x_copy(p, 0, q).wait_send()
        for core in range(2):
            (whole_copy(core) if p == whole else back_copy(p, core)).wait_send()
        for d in range(1, ctx_count):
            if p != whole:
                part_copy(p, d).wait_send()


def write_kernel(weights_grad, states_grad, keys_grad, values_grad, weights_out, states_out, keys_out, values_out, sem):
    pairs = (
        (weights_grad, weights_out), (states_grad, states_out), (keys_grad, keys_out), (values_grad, values_out),
    )
    copies = [pltpu.make_async_copy(source, target, sem.at[n]) for n, (source, target) in enumerate(pairs)]
    for copy in copies:
        copy.start()
    for copy in copies:
        copy.wait()


def on_device(
    states, out_grad, doc_keys, doc_values, norm_gain, expert_ids, gate_values, expert_weights
):
    tokens, model_width = states.shape[1:]
    key_count = doc_keys.shape[1]
    ctx_count, experts = lax.axis_size("ctx"), lax.axis_size("exp")
    chips = experts // 2
    hidden = expert_weights.shape[1]
    capacity = 8 * -(-5 * TOP * tokens // (32 * experts))
    pair = 2 * capacity
    slot_rows = experts * capacity
    tiles = model_width // HEAD
    width = HEAD * max(-(-(c + 1) * tiles // ctx_count) - c * tiles // ctx_count for c in range(ctx_count))
    order = [0] + sorted(range(1, chips), key=lambda j: min(j, chips - j))
    pieces = 2
    groups = [[0, 1]] + [[p] for p in range(2, chips)]
    vmem = pl.BlockSpec(memory_space=pltpu.VMEM)
    hbm = pl.BlockSpec(memory_space=pltpu.HBM)
    shape = jax.ShapeDtypeStruct
    dma = pltpu.SemaphoreType.DMA
    near = max(chips - 1, 1)
    scratch = [
        ((2, slot_rows, model_width), BF16),
        ((slot_rows, hidden), BF16),
        ((slot_rows, hidden), BF16),
        ((tokens, model_width), BF16),
        ((tokens, model_width), BF16),
        ((key_count, model_width), BF16),
        ((key_count, model_width), BF16),
        ((hidden, 2, model_width), BF16),
        ((hidden, model_width), BF16),
        ((hidden, model_width), BF16),
        ((2, tokens, model_width), BF16),
        ((experts, tokens), F32),
        ((experts, tokens), F32),
        ((near, capacity, model_width), BF16),
        ((2, capacity, model_width), BF16),
        ((2, chips, 2, capacity, model_width), BF16),
        ((slot_rows, model_width), BF16),
        ((2, capacity, model_width), BF16),
        ((2, capacity, model_width), BF16),
        ((pair, model_width), BF16),
        ((near, 2, capacity, tokens), BF16),
        ((2, pair, tokens), BF16),
        ((tokens, model_width), F32),
        ((tokens, model_width), BF16),
        ((3, HEADS, tokens), F32),
        ((ctx_count - 1, 3, HEADS, tokens), F32),
        ((3, HEADS, tokens), F32),
        ((near, ctx_count - 1, pair, width), BF16),
        ((near, 2, capacity, width), BF16),
        ((near, 2, capacity, width), BF16),
        ((ctx_count - 1, tokens, width), BF16),
        ((ctx_count, tokens, width), BF16),
        ((tokens, model_width), BF16),
    ]
    semaphores = [
        (5,),
        (2, chips, pieces),
        (2, 2),
        (2, chips, max(ctx_count // 2, 3), pieces),
        (2, chips, ctx_count // 2 + 1, pieces),
        (2, ctx_count - 1),
        (2, 1),
        (2, 2),
        (2, chips, ctx_count - 1),
        (2, chips, 2),
        (2, ctx_count - 1, 2),
        (2, 4, ctx_count // 2, 2),
    ]
    weights_grad, keys_grad, values_grad, states_grad = pl.pallas_call(
        functools.partial(block_kernel, ctx_count, experts, order, groups, pieces, 1),
        out_shape=(
            shape((hidden, 2, model_width), BF16),
            shape((key_count, model_width), BF16),
            shape((key_count, model_width), BF16),
            shape((tokens, model_width), BF16),
        ),
        in_specs=[vmem] * 3 + [hbm] * 5,
        out_specs=(vmem,) * 4,
        scratch_shapes=[pltpu.VMEM(s, t) for s, t in scratch] + [dma(s) for s in semaphores],
        compiler_params=pltpu.CompilerParams(
            vmem_limit_bytes=VMEM_LIMIT, collective_id=0, has_side_effects=True
        ),
    )(
        *(pltpu.with_memory_space_constraint(a, pltpu.HBM) for a in (norm_gain, expert_ids[0].T, gate_values[0].T)),
        *(pltpu.with_memory_space_constraint(a, pltpu.HBM) for a in (states[0], out_grad[0], doc_keys[0], doc_values[0], expert_weights[0])),
    )
    weights_grad, states_grad, keys_grad, values_grad = pl.pallas_call(
        write_kernel,
        out_shape=(
            shape((hidden, 2, model_width), BF16),
            shape((tokens, model_width), BF16),
            shape((key_count, model_width), BF16),
            shape((key_count, model_width), BF16),
        ),
        in_specs=[vmem] * 4,
        out_specs=(hbm,) * 4,
        scratch_shapes=[
            dma((4,)),
        ],
        compiler_params=pltpu.CompilerParams(vmem_limit_bytes=SECOND_LIMIT),
    )(weights_grad, states_grad, keys_grad, values_grad)
    return states_grad[None], keys_grad[None], values_grad[None], weights_grad[None]


def solution(mesh):
    return jax.shard_map(
        on_device,
        mesh=mesh,
        in_specs=(
            P("exp", None, None),
            P("exp", None, None),
            P("exp", "ctx", None),
            P("exp", "ctx", None),
            P(),
            P("exp", None, None),
            P("exp", None, None),
            P("exp", "ctx", None, None),
        ),
        out_specs=(
            P("exp", None, None),
            P("exp", "ctx", None),
            P("exp", "ctx", None),
            P("exp", "ctx", None, None),
        ),
        check_vma=False,
    )
```
